32 devices in a mesh: gx: 8 (over y, x, core), gy: 4 (over z).
Axes of the slice: x: 2, y: 2, z: 4, core: 2. Of those that a mesh axis runs over, the one named last changes fastest.
Arguments:
- state: bfloat16 [32, 12, 192, 256], P('gx', 'gy'), may hold values from -1 to 1
- weights: bfloat16 [32, 12, 9, 256, 256], P('gx', 'gy'), may hold values from -0.125 to 0.125
- drive: bfloat16 [2, 32, 12, 192, 256], P(None, 'gx', 'gy'), may hold values from -6 to 6
- leak: float32 [32, 12, 256], P('gx', 'gy'), may hold values from 0.1 to 1
- link_dev: int32 [8, 4, 12, 3], P(None, 'gy'), may hold values from 0 to 7, all different within a row; in each aligned block of 12 rows (0 to 11, 12 to 23, ..., all dimensions but the last counted through in order) at most 6 rows name the same one
- link_blk: int32 [8, 4, 12, 3], P(None, 'gy'), may hold values from 0 to 11
- offsets: int32 [5, 2], replicated, may hold values from -1 to 1, as said below
- gram_prev: float32 [32, 12, 256, 256], P('gx', 'gy'), may hold values from -6 to 6
Outputs:
- final_state: bfloat16 [32, 12, 192, 256], P('gx', 'gy')
- gram: float32 [32, 12, 256, 256], P('gx', 'gy')
The draws below stay inside these ranges and needn't reach their ends.
Inputs may be any that keep to these rules, and one draw needn't show every extreme that they name: `link_dev`: the 3 sources of one block lie on different indices of gx; among the blocks of one device at most 6 sources lie on any one index of gx, and exactly 6 on some. Five distinct offsets.
All inputs are finite; a program needn't handle non-finite values.
Results may differ from the reference program's by a relative error of at most 0.0046.
Values may be sent and summed in bfloat16 or wider, within the bound.
A program may use at most 192 MiB of HBM per device.

```python
import math
import jax
import jax.numpy as jnp
import numpy as np
from jax import lax

U = 256
LINKS = 3
STENCIL = 5
STEPS = 2
R = 4
C = 3
SEQ = 192
CAP = 6
NBR = 32
NBC = 12
N_GX = 8
N_GY = 4


def draw_offsets(key, part):
    chosen = jax.random.permutation(key, 9)[:STENCIL]
    return jnp.stack([chosen // 3 - 1, chosen % 3 - 1], axis=1).astype(jnp.int32)


def place_ends(drawn, stream_key, smallest, top_value):
    extent = drawn.shape
    place = [jax.random.randint(jax.random.fold_in(stream_key, axis), (), 0, extent[axis]) for axis in range(len(extent))]
    drawn = drawn.at[tuple(place)].set(smallest)
    longest = extent.index(max(extent))
    place[longest] = (place[longest] + 1) % extent[longest]
    return drawn.at[tuple(place)].set(top_value)


def levels(rng, extent, split, smallest, high):
    loudness, own = 1.0, jax.random.fold_in(rng, 6)
    for position, shards_of in split:
        steps = jnp.exp(jax.random.uniform(jax.random.fold_in(own, position), (shards_of,), jnp.float32, smallest / len(split), high / len(split)))
        loudness = loudness * jnp.repeat(steps, extent[position] // shards_of).reshape([-1 if axis == position else 1 for axis in range(len(extent))])
    return loudness


def routed_block(key, own, number, rows, number_of, top, most, slope):
    sequence = jax.random.permutation(key, number_of)
    packed, common = portions_of(number_of, rows * top, most, slope, True), portions_of(number_of, rows * top, most, slope, False)
    places = jnp.arange(number_of)

    def named(sizes, turn):
        used = int((sizes > 0).sum())
        fixed = max(1, used // 4)
        passed = fixed + (places - fixed + turn * (used - fixed)) % max(1, number_of - fixed)
        return jnp.zeros((number_of,), jnp.int32).at[sequence[jnp.where(places < fixed, places, passed)]].set(jnp.asarray(sizes, jnp.int32))

    sizes = jnp.where(number % 4 == 0, named(packed, number // 4), named(common, number - number // 4 - 1))
    mixed = jax.random.permutation(jax.random.fold_in(own, 3), number_of)
    giver, taker = mixed[0:number_of // 2 * 2:2], mixed[1:number_of // 2 * 2:2]
    room = jnp.minimum(sizes[giver] - 1, most - sizes[taker]) // 2
    room = jnp.where((giver == sequence[0]) | (taker == sequence[0]) | (sizes[taker] == 0), 0, jnp.maximum(room, 0))
    passed = jax.random.randint(jax.random.fold_in(own, 4), (number_of // 2,), 0, 1 << 20) % (room + 1)
    sizes = sizes.at[giver].add(-passed).at[taker].add(passed)
    labels = jnp.searchsorted(jnp.cumsum(sizes), jnp.arange(rows * top), side="right").astype(jnp.int32)
    listing = labels.reshape(top, rows).T
    listing = listing[jax.random.permutation(jax.random.fold_in(own, 1), rows)]
    turn = jax.random.randint(jax.random.fold_in(own, 2), (rows, 1), 0, top)
    return jnp.take_along_axis(listing, (jnp.arange(top)[None, :] + turn) % top, axis=1)


def portions_of(amount, total, limit, slope, full):
    loads = [(1 << 20) // math.isqrt(rank ** slope) + 1 for rank in range(1, amount + 1)]
    largest = limit if full else min(limit, max(-(-total // amount), total * loads[0] // sum(loads)))
    least = 1 if total - largest >= amount - 1 else 0
    counts, surplus = [largest] + [least] * (amount - 1), total - largest - least * (amount - 1)
    while surplus > 0:
        movable = [i for i in range(1, amount) if counts[i] < largest] or [i for i in range(1, amount) if counts[i] < limit]
        mass, budget = sum([loads[i] for i in movable]), surplus
        for i in movable:
            extra = min(limit - counts[i], max(1, budget * loads[i] // mass), surplus)
            counts[i] = counts[i] + extra
            surplus = surplus - extra
    return np.array(counts)


def bell_draw(stream_key, dims, spread, reach, split=(), kind=jnp.bfloat16):
    result = spread * jax.random.normal(stream_key, dims, jnp.float32)
    if split:
        result = result * levels(stream_key, dims, split, -0.22, 0.18)
    return jnp.clip(result, -reach, reach).astype(kind)


def setup_inputs(seed: int = 0) -> dict:
    keys = jax.random.split(jax.random.key(seed), 9)
    state = jnp.clip(jax.random.uniform(keys[0], (NBR, NBC, SEQ, U), jnp.float32, -1.0, 1.0) * levels(keys[0], (NBR, NBC, SEQ, U), ((0, 8), (1, 4)), -0.4, 0.0), -1.0, 1.0).astype(jnp.bfloat16)
    weights = bell_draw(keys[1], (NBR, NBC, STENCIL + LINKS + 1, U, U), ((STENCIL + LINKS + 1) * U) ** -0.5, 0.125, ((0, 8), (1, 4)))
    drive = bell_draw(keys[2], (STEPS, NBR, NBC, SEQ, U), 1.0, 6.0, ((1, 8), (2, 4)))
    leak = jnp.clip(jnp.exp(math.log(1.0) - 2.3025851 * jax.random.uniform(keys[3], (NBR, NBC, U), jnp.float32) ** levels(keys[3], (NBR, NBC, U), ((0, 8), (1, 4)), -0.2, 0.2)), 0.1, 1.0)
    link_dev_keys = jax.random.split(jax.random.fold_in(keys[4], 1), N_GX * N_GY * (R * C) // (R * C))
    link_dev_turns = jax.random.permutation(jax.random.fold_in(keys[4], 3), N_GX * N_GY * (R * C) // (R * C))
    link_dev = jax.vmap(lambda own, number: routed_block(jax.random.fold_in(keys[4], 2), own, number, R * C, N_GX, LINKS, CAP, 2))(link_dev_keys, link_dev_turns).reshape((N_GX, N_GY, R * C, LINKS))
    link_blk = place_ends(jax.random.randint(keys[5], (N_GX, N_GY, R * C, LINKS), 0, R * C), jax.random.fold_in(keys[5], 1), 0, (R * C) - 1).astype(jnp.int32)
    offsets = draw_offsets(jax.random.fold_in(keys[8], 71), 0)
    gram_prev = bell_draw(keys[7], (NBR, NBC, U, U), 1.0, 6.0, ((0, 8), (1, 4)), jnp.float32)
    return dict(state=state, weights=weights, drive=drive, leak=leak, link_dev=link_dev, link_blk=link_blk, offsets=offsets, gram_prev=gram_prev)


def reference(state, weights, drive, leak, link_dev, link_blk, offsets, gram_prev):
    dev_grid = link_dev.reshape(N_GX, N_GY, R, C, LINKS).transpose(0, 2, 1, 3, 4).reshape(NBR, NBC, LINKS)
    blk_grid = link_blk.reshape(N_GX, N_GY, R, C, LINKS).transpose(0, 2, 1, 3, 4).reshape(NBR, NBC, LINKS)
    col_band = (jnp.arange(NBC, dtype=jnp.int32) // C)[None, :, None]
    src_row = (dev_grid * R + blk_grid // C).astype(jnp.int32)
    src_col = (col_band * C + blk_grid % C).astype(jnp.int32)
    current = state
    gram = gram_prev
    for step_id in range(STEPS):
        padded = jnp.pad(current, ((1, 1), (1, 1), (0, 0), (0, 0)))

        def one_row(row_id):
            w_row = lax.dynamic_index_in_dim(weights, row_id, 0, keepdims=False)
            preact = jnp.zeros((NBC, SEQ, U), jnp.float32)
            for offset_id in range(STENCIL):
                start_r = (row_id + 1 + offsets[offset_id, 0]).astype(jnp.int32)
                start_c = (1 + offsets[offset_id, 1]).astype(jnp.int32)
                zero = jnp.zeros((), jnp.int32)
                nearby = lax.dynamic_slice(padded, (start_r, start_c, zero, zero), (1, NBC, SEQ, U))[0]
                preact = preact + jnp.einsum("csu,cuv->csv", nearby.astype(jnp.float32), w_row[:, offset_id].astype(jnp.float32))
            sources = current[src_row[row_id], src_col[row_id]]
            preact = preact + jnp.einsum("clsu,cluv->csv", sources.astype(jnp.float32), w_row[:, STENCIL:STENCIL + LINKS].astype(jnp.float32))
            inputs = lax.dynamic_index_in_dim(drive[step_id], row_id, 0, keepdims=False)
            preact = preact + jnp.einsum("csu,cuv->csv", inputs.astype(jnp.float32), w_row[:, STENCIL + LINKS].astype(jnp.float32))
            old_row = lax.dynamic_index_in_dim(current, row_id, 0, keepdims=False).astype(jnp.float32)
            rate = lax.dynamic_index_in_dim(leak, row_id, 0, keepdims=False)[:, None, :]
            fresh = ((1.0 - rate) * old_row + rate * jnp.tanh(preact)).astype(jnp.bfloat16)
            fresh_wide = fresh.astype(jnp.float32)
            return fresh, jnp.einsum("csu,csv->cuv", fresh_wide, fresh_wide)

        fresh_all, gram_terms = lax.map(one_row, jnp.arange(NBR, dtype=jnp.int32))
        current = fresh_all
        gram = gram + gram_terms
    return current, gram
```

```python
import functools

import jax
import jax.numpy as jnp
from jax import lax
from jax.experimental import pallas as pl
from jax.experimental.pallas import tpu as pltpu
from jax.sharding import PartitionSpec as P

MESH = pl.DeviceIdType.MESH
PART, ALONG_X, ALONG_Y, X_PART, Y_PART, DIAG, D_PART = range(7)


def padded(x, sides, width):
    for axis, dim in sides:
        size, length = (lax.axis_size(axis), x.shape[dim])
        up = [(i, (i + 1) % size) for i in range(size - 1)]
        down = [(j, i) for i, j in up]
        last = lax.slice_in_dim(x, length - width, length, axis=dim)
        first = lax.slice_in_dim(x, 0, width, axis=dim)
        before = lax.ppermute(last, axis, up)
        after = lax.ppermute(first, axis, down)
        x = jnp.concatenate([before, x, after], axis=dim)
    return x


def shards(state, weights, drive, leak, link_dev, link_blk, offsets, gram_prev):
    grid_rows, grid_cols, batch_cols, units = state.shape
    nblocks = grid_rows * grid_cols
    nlinks = link_dev.shape[-1]
    nstencil = offsets.shape[0]
    gx_size = lax.axis_size("gx")
    own_index = lax.axis_index("gx")
    all_dev = link_dev[:, 0].reshape(gx_size, nblocks * nlinks)
    all_blk = link_blk[:, 0].reshape(gx_size, nblocks * nlinks)
    my_dev = lax.dynamic_index_in_dim(all_dev, own_index, 0, keepdims=False)
    my_blk = lax.dynamic_index_in_dim(all_blk, own_index, 0, keepdims=False)
    w_long = weights[:, :, nstencil : nstencil + nlinks].reshape(nblocks, nlinks, units, units)
    current = state
    gram = gram_prev
    for step_id in range(drive.shape[0]):
        extended = padded(current, (("gx", 0), ("gy", 1)), 1)
        preact = jnp.zeros((grid_rows, grid_cols, batch_cols, units), jnp.float32)
        for offset_id in range(nstencil):
            zero = jnp.zeros((), jnp.int32)
            start_r = 1 + offsets[offset_id, 0]
            start_c = 1 + offsets[offset_id, 1]
            nearby = lax.dynamic_slice(
                extended, (start_r, start_c, zero, zero), (grid_rows, grid_cols, batch_cols, units)
            )
            preact = preact + jnp.einsum(
                "rcsu,rcuv->rcsv",
                nearby,
                weights[:, :, offset_id],
                preferred_element_type=jnp.float32,
            )
        flat_state = current.reshape(nblocks, batch_cols, units)
        whole = lax.all_gather(flat_state[None], "gx", axis=0, tiled=True)
        picked = whole.reshape(gx_size * nblocks, batch_cols, units)[my_dev * nblocks + my_blk]
        picked = picked.reshape(nblocks, nlinks, batch_cols, units)
        distant = jnp.einsum("blsu,bluv->bsv", picked, w_long, preferred_element_type=jnp.float32)
        preact = preact + distant.reshape(grid_rows, grid_cols, batch_cols, units)
        preact = preact + jnp.einsum(
            "rcsu,rcuv->rcsv",
            drive[step_id],
            weights[:, :, nstencil + nlinks],
            preferred_element_type=jnp.float32,
        )
        rate = leak[:, :, None, :]
        current = ((1.0 - rate) * current.astype(jnp.float32) + rate * jnp.tanh(preact)).astype(
            jnp.bfloat16
        )
        gram = gram + jnp.einsum(
            "rcsu,rcsv->rcuv", current, current, preferred_element_type=jnp.float32
        )
    return (current, gram)


def reservoir(
    n_gy, state, w, drive, leak, ldev, lblk, offs, gprev, out, gout,
    gath00, gath01, gath10, gath11, ext00, ext01, ext10, ext11, wv, dv, gv, acc, xf,
    load_sem, store_sem, send_sem, recv_sem, zsend_sem, zrecv_sem,
):
    rows, cols, seq, units = state.shape
    nstencil, nlinks = offs.shape[1], ldev.shape[1]
    half = seq // 2
    g, b = lax.axis_index("gx"), lax.axis_index("gy")
    core, x, y = lax.rem(g, 2), lax.rem(lax.div(g, 2), 2), lax.div(g, 4)
    near = lambda fy, fx, fc: (
        (1 - y if fy else y) * 4 + (1 - x if fx else x) * 2 + (1 - core if fc else core)
    )
    ids = {
        PART: near(0, 0, 1), ALONG_X: near(0, 1, 0), ALONG_Y: near(1, 0, 0),
        X_PART: near(0, 1, 1), Y_PART: near(1, 0, 1), DIAG: near(1, 1, 0), D_PART: near(1, 1, 1),
    }
    has_left, has_right = b > 0, b < n_gy - 1
    has_up, has_down = g > 0, g < 7
    gaths, exts = (gath00, gath01, gath10, gath11), (ext00, ext01, ext10, ext11)

    loads = []

    def load(src, dst):
        copy = pltpu.make_async_copy(src, dst, load_sem.at[len(loads)])
        copy.start()
        loads.append(copy)
        return copy

    for r in range(rows):
        for s in (0, 1):
            load(state.at[r, :, pl.ds(s * half, half)], gaths[s].at[g, pl.ds(r * cols, cols)])

    barrier = pltpu.get_barrier_semaphore()
    for rel in (PART, ALONG_X, ALONG_Y):
        pl.semaphore_signal(barrier, inc=1, device_id={"gx": ids[rel]}, device_id_type=MESH)

    @pl.when(has_left)
    def _():
        pl.semaphore_signal(barrier, inc=1, device_id={"gy": b - 1}, device_id_type=MESH)

    @pl.when(has_right)
    def _():
        pl.semaphore_signal(barrier, inc=1, device_id={"gy": b + 1}, device_id_type=MESH)

    inside = jnp.logical_and(has_left, has_right)

    @pl.when(inside)
    def _():
        pl.semaphore_wait(barrier, 5)

    @pl.when(jnp.logical_not(inside))
    def _():
        pl.semaphore_wait(barrier, 4 if n_gy > 1 else 3)

    sends = []

    def send(t, rel_from, r, to, rel_there):
        origin = g if rel_from is None else ids[rel_from]
        here = gaths[t].at[origin, pl.ds(r * cols, cols)]
        src = state.at[r, :, pl.ds(t * half, half)] if rel_from is None and t < 2 else here
        copy = pltpu.make_async_remote_copy(
            src_ref=src, dst_ref=here,
            send_sem=send_sem.at[len(sends)], recv_sem=recv_sem.at[t, rel_there, r],
            device_id={"gx": ids[to]}, device_id_type=MESH,
        )
        copy.start()
        sends.append(copy)

    def send_own(t, r, to):
        send(t, None, r, to, to)

    def arrived(t, rel, r):
        here = gaths[t].at[ids[rel], pl.ds(r * cols, cols)]
        pltpu.make_async_remote_copy(
            src_ref=here, dst_ref=here,
            send_sem=send_sem.at[0], recv_sem=recv_sem.at[t, rel, r],
            device_id={"gx": ids[PART]}, device_id_type=MESH,
        ).wait_recv()

    def relay(t, rel, r, across=None):
        arrived(t, rel, r)
        if across is not None:
            send(t, rel, r, across, DIAG)
        send(t, rel, r, PART, {ALONG_X: X_PART, ALONG_Y: Y_PART, DIAG: D_PART}[rel])

    def rim_copy(t, side, kind):
        col = 0 if side == 0 else cols - 1
        there = cols + 1 if side == 0 else 0
        gath, ext = gaths[t], exts[t]
        if kind == 0:
            return [
                pltpu.make_async_remote_copy(
                    src_ref=state.at[r, col, pl.ds(t * half, half)]
                    if t < 2
                    else gath.at[g, r * cols + col],
                    dst_ref=ext.at[r + 1, there],
                    send_sem=zsend_sem.at[t, side, r], recv_sem=zrecv_sem.at[t, side, r],
                    device_id={"gy": b - 1 if side == 0 else b + 1}, device_id_type=MESH,
                )
                for r in range(rows)
            ]
        src = (
            gath.at[lax.rem(g + 7, 8), (rows - 1) * cols + col]
            if kind == 1
            else gath.at[lax.rem(g + 1, 8), col]
        )
        return [
            pltpu.make_async_remote_copy(
                src_ref=src,
                dst_ref=ext.at[0 if kind == 1 else rows + 1, there],
                send_sem=zsend_sem.at[t, side, rows + kind - 1],
                recv_sem=zrecv_sem.at[t, side, rows + kind - 1],
                device_id={"gy": b - 1 if side == 0 else b + 1}, device_id_type=MESH,
            )
        ]

    def rims(t, do, kinds):
        for side in (0, 1):
            present = (has_left, has_right)
            who = present[side] if do != "wait_recv" else present[1 - side]
            for kind in kinds:
                cond = who
                if kind == 1:
                    cond = jnp.logical_and(who, has_up)
                if kind == 2:
                    cond = jnp.logical_and(who, has_down)

                @pl.when(cond)
                def _():
                    for copy in rim_copy(t, side, kind):
                        getattr(copy, do)()

    def begin(t, r):
        if r != 2:
            send_own(t, r, ALONG_X)
        if r != 1:
            send_own(t, r, ALONG_Y)
        send_own(t, r, PART)

    def exchange(t):
        relay(t, ALONG_X, 0, ALONG_Y)
        send_own(t, 1, ALONG_Y)
        relay(t, ALONG_Y, 0)
        relay(t, ALONG_X, 3)
        relay(t, ALONG_Y, 3, ALONG_X)
        send_own(t, 2, ALONG_X)
        relay(t, ALONG_X, 1, ALONG_Y)
        relay(t, ALONG_Y, 2, ALONG_X)

    def borders(t):
        relay(t, DIAG, 0)
        relay(t, DIAG, 3)
        for rel in (PART, X_PART, D_PART):
            arrived(t, rel, 0)
            arrived(t, rel, 3)
        rims(t, "start", (1, 2))
        fill(t)
        rims(t, "wait_recv", (0, 1, 2))

    def finish(t):
        relay(t, ALONG_Y, 1)
        relay(t, ALONG_X, 2)
        relay(t, DIAG, 1)
        relay(t, DIAG, 2)
        for rel in (PART, X_PART, D_PART):
            arrived(t, rel, 1)
            arrived(t, rel, 2)
        for r in range(rows):
            arrived(t, Y_PART, r)

    def fill(t):
        gath, ext = gaths[t], exts[t]

        def place(i, carry):
            r, c = i // cols, lax.rem(i, cols)
            ext[r + 1, c + 1] = gath[g, i]
            return carry

        lax.fori_loop(0, rows * cols, place, 0)
        zero = jnp.zeros((half, units), jnp.bfloat16)

        @pl.when(has_up)
        def _():
            for c in range(cols):
                ext[0, c + 1] = gath[lax.rem(g + 7, 8), (rows - 1) * cols + c]

        @pl.when(has_down)
        def _():
            for c in range(cols):
                ext[rows + 1, c + 1] = gath[lax.rem(g + 1, 8), c]

        for there, edge in ((0, has_up), (rows + 1, has_down)):

            @pl.when(jnp.logical_not(edge))
            def _():
                for c in range(cols + 2):
                    ext[there, c] = zero

        for there, side in ((0, has_left), (cols + 1, has_right)):

            @pl.when(jnp.logical_not(side))
            def _():
                for r in range(rows):
                    ext[r + 1, there] = zero
                for r, edge in ((0, has_up), (rows + 1, has_down)):

                    @pl.when(edge)
                    def _():
                        ext[r, there] = zero

    def dot(a, weight):
        return jnp.dot(a, weight, preferred_element_type=jnp.float32)

    def nearby(t):
        ext = exts[t]

        def one(i, carry):
            r, c = i // cols, lax.rem(i, cols)
            total = dot(
                dv[t // 2, r, c, pl.ds(t % 2 * half, half)], wv[r, c, nstencil + nlinks]
            )
            for k in range(nstencil):
                total = total + dot(ext[r + 1 + offs[0, k], c + 1 + offs[1, k]], wv[r, c, k])
            acc[i] = total
            return carry

        lax.fori_loop(0, rows * cols, one, 0)

    def gram_of(r, c, now):
        gv[r, c] += lax.dot_general(
            now, now, (((0,), (0,)), ((), ())), preferred_element_type=jnp.float32
        )

    def distant(t, r):
        gath = gaths[t]

        def one(c, carry):
            i = r * cols + c
            total = acc[i]
            for l in range(nlinks):
                total = total + dot(gath[ldev[g, l, 0, i], lblk[g, l, 0, i]], wv[r, c, nstencil + l])
            rate = leak[c, pl.ds(r, 1), :]
            old = gath[g, i].astype(jnp.float32)
            now = ((1.0 - rate) * old + rate * jnp.tanh(total)).astype(jnp.bfloat16)
            if t >= 2:
                xf[i, pl.ds((t - 2) * half, half)] = now
            else:
                gaths[t + 2][g, i] = now
                gram_of(r, c, now)
            return carry

        lax.fori_loop(0, cols, one, 0)

    order = (0, 3, 1, 2)

    def start(t):
        for r in order:
            begin(t, r)
        rims(t, "start", (0,))

    stores = []

    def store(src, dst):
        copy = pltpu.make_async_copy(src, dst, store_sem.at[len(stores)])
        copy.start()
        stores.append(copy)

    start(0)
    for r in range(rows):
        load(w.at[r], wv.at[r])
    load(drive, dv)
    load(gprev, gv)
    for t in range(4):
        exchange(t)
        if t < 3:
            start(t + 1)
        if t == 0:
            for copy in loads:
                copy.wait()
        borders(t)
        nearby(t)
        finish(t)
        for r in range(rows):
            distant(t, r)
            if t == 3:
                store(xf.at[pl.ds(r * cols, cols)], out.at[r])
        if t == 1:
            store(gv, gout)
    for copy in sends:
        copy.wait_send()
    for t in range(4):
        rims(t, "wait_send", (0, 1, 2))
    for copy in stores:
        copy.wait()


def closing(x, gram, out, gout, xv, gv, x_sem, g_sem, out_sem, gout_sem):
    rows, cols = x.shape[:2]
    copy = pltpu.make_async_copy
    x_in = [copy(x.at[r], xv.at[r], x_sem.at[r]) for r in range(rows)]
    g_in = [copy(gram.at[r], gv.at[r], g_sem.at[r]) for r in range(rows)]
    x_out = [copy(xv.at[r], out.at[r], out_sem.at[r]) for r in range(rows)]
    g_out = [copy(gv.at[r], gout.at[r], gout_sem.at[r]) for r in range(rows)]
    for r in range(rows):
        x_in[r].start()
        g_in[r].start()
    for r in range(rows):
        x_in[r].wait()
        x_out[r].start()
        g_in[r].wait()
        for c in range(cols):
            now = xv[r, c]
            gv[r, c] += lax.dot_general(
                now, now, (((0,), (0,)), ((), ())), preferred_element_type=jnp.float32
            )
        g_out[r].start()
    for r in range(rows):
        x_out[r].wait()
        g_out[r].wait()


SLOTS, FIRST, AHEAD = 13, 8, 5
LATE = SLOTS - FIRST
LANES = 16


def route(ldev, lblk, spot, pick, fits):
    rows_of = lambda n: lax.broadcasted_iota(jnp.int32, (n, 128), 0)
    lanes_of = lambda n: lax.broadcasted_iota(jnp.int32, (n, 128), 1)
    nlinks, nblocks = ldev.shape[1], ldev.shape[3]
    g = lax.axis_index("gx")
    core, home = g % 2, g // 2
    lane = lanes_of(8)
    chip, block = lane // 32, lane % LANES

    needs = []
    for c in range(4):
        need = jnp.zeros((8, 128), jnp.bool_)
        for a in (2 * c, 2 * c + 1):
            for l in range(nlinks):
                for q in range(nblocks):
                    need = need | (lane == ldev[a, l, 0, q] * LANES + lblk[a, l, 0, q])
        for src, dst in ((2 * c - 1, 2 * c), (2 * c + 2, 2 * c + 1)):
            if 0 <= src < 8:
                first = nblocks - 3 if src < dst else 0
                need = need | ((lane >= src * LANES + first) & (lane < src * LANES + first + 3))
        needs.append(need.astype(jnp.int32))

    def seen(flip):
        return jnp.where(
            chip == 0, needs[flip],
            jnp.where(chip == 1, needs[1 ^ flip], jnp.where(chip == 2, needs[2 ^ flip], needs[3 ^ flip])),
        )

    nx, ny, nd = seen(1), seen(2), seen(3)
    only_x, both, neither, only_y = nd * nx * (1 - ny), nd * nx * ny, nd * (1 - nx) * (1 - ny), nd * ny * (1 - nx)
    classes = [only_x, both, neither, only_y, nx, ny]

    def stack(parts):
        sub, stacked = rows_of(8), jnp.zeros((8, 128), jnp.int32)
        for k, part in enumerate(parts):
            stacked = jnp.where(sub == k, part, stacked)
        return stacked.astype(jnp.float32)

    def times(x, matrix):
        return jnp.dot(
            x.astype(jnp.bfloat16), matrix.astype(jnp.float32).astype(jnp.bfloat16),
            preferred_element_type=jnp.float32,
        ).astype(jnp.int32)

    above, across = rows_of(128), lanes_of(128)
    upto = (above <= across) & (above // 32 == across // 32)
    counted = stack(classes)
    sums = times(counted, upto)
    totals = [times(counted, above // 32 == c) for c in range(4)]
    row = lambda x, k: jnp.broadcast_to(x[k : k + 1], (8, 128))

    cand = rows_of(32) * 128 + lanes_of(32)
    wide = lambda c, k: jnp.broadcast_to(totals[c][k : k + 1], (32, 128))
    fx, fy, rx, ry = [], [], [], []

    def passed(counts, digit):
        total = counts[0] + counts[1] + counts[2] + counts[3]
        start = (2 * counts[0] + counts[1] + counts[2] + 1) // 2 - 4
        return total, jnp.maximum(jnp.minimum(start + digit, total), 0)

    for c in range(4):
        counts = [wide(c, k) for k in range(6)]
        total, m = passed(counts, (cand >> (3 * c)) & 7)
        rest = total - m
        rx.append(m)
        ry.append(rest)
        fx.append(counts[4] + jnp.maximum(m - counts[0] - counts[1], 0))
        fy.append(
            counts[5] + jnp.maximum(jnp.minimum(rest - counts[3], counts[2]), 0)
            + jnp.maximum(rest - counts[3] - counts[2] - counts[1], 0)
        )
    worst = jnp.zeros((32, 128), jnp.int32)
    for c in range(4):
        worst = jnp.maximum(worst, jnp.maximum(fx[c], 2 * FIRST) + ry[c ^ 2])
        worst = jnp.maximum(worst, jnp.maximum(fy[c], 2 * FIRST) + rx[c ^ 1])
        worst = jnp.where(jnp.maximum(rx[c], ry[c]) > 2 * AHEAD, 255, worst)
    best = jnp.min(worst * 4096 + cand)
    fits[...] = jnp.where(jnp.zeros((8, 128), jnp.int32) + best // 4096 <= 2 * SLOTS, 1, 0)

    pickc = lambda values: jnp.where(
        chip == 0, values[0], jnp.where(chip == 1, values[1], jnp.where(chip == 2, values[2], values[3]))
    )
    count = [pickc([row(totals[c], k) for c in range(4)]) for k in range(6)]
    digit = pickc([(best >> (3 * c)) & 7 for c in range(4)])
    total, m = passed(count, digit)
    rank = jnp.where(
        only_x > 0, row(sums, 0) - 1,
        jnp.where(
            both > 0, count[0] + row(sums, 1) - 1,
            jnp.where(
                neither > 0, count[0] + count[1] + row(sums, 2) - 1,
                count[0] + count[1] + count[2] + row(sums, 3) - 1,
            ),
        ),
    )
    via_x = jnp.where(rank < m, nd, 0)
    via_y = nd - via_x
    more = times(stack([nx * (1 - via_x), ny * (1 - via_y)]), upto)
    over = rank - m
    pos_x = jnp.where(via_x > 0, rank, m + row(more, 0) - 1)
    pos_y = jnp.where(via_y > 0, over, total - m + row(more, 1) - 1)
    held_x, held_y = jnp.maximum(nx, via_x), jnp.maximum(ny, via_y)

    mine = block + jnp.where((lane // LANES) % 2 == core, 0, 12)
    base = 2 * nblocks
    inward = lambda link, k, p: base + 2 * SLOTS * link + jnp.where(k == core, 0, SLOTS) + p
    odd = lambda x: x & 1
    there = jnp.where(
        chip == home, mine,
        jnp.where(
            chip == (home ^ 1), inward(0, odd(pos_x), pos_x >> 1),
            jnp.where(
                chip == (home ^ 2), inward(1, odd(pos_y + 1), pos_y >> 1),
                jnp.where(
                    via_x > 0, inward(1, odd(rank), SLOTS - 1 - (rank >> 1)),
                    inward(0, odd(over + 1), SLOTS - 1 - (over >> 1)),
                ),
            ),
        ),
    )
    spot[...] = jnp.maximum(jnp.minimum(there, base + 4 * SLOTS - 1), 0)

    sub = rows_of(32)
    place, is_y = sub % 16, sub >= 16
    full = lambda x: jnp.broadcast_to(x[0:1], (32, 128))
    own_chip = full(jnp.where(chip == home, 1, 0)) > 0
    own_at = jnp.where(is_y, full(pos_y), full(pos_x))
    own_core = jnp.where(is_y, odd(own_at + 1), odd(own_at))
    own_held = jnp.where(is_y, full(held_y), full(held_x)) > 0
    own_hit = own_chip & own_held & (own_at >> 1 == place) & (own_core == core)
    pass_x = full(jnp.where(chip == (home ^ 2), via_y, 0))
    pass_y = full(jnp.where(chip == (home ^ 1), via_x, 0))
    pass_held = jnp.where(is_y, pass_y, pass_x) > 0
    pass_rank = jnp.where(is_y, full(rank), full(over))
    pass_core = jnp.where(is_y, odd(pass_rank), odd(pass_rank + 1))
    pass_hit = pass_held & (SLOTS - 1 - (pass_rank >> 1) == place) & (pass_core == core)
    value = jnp.where(own_hit, full(mine), 0) + jnp.where(pass_hit, base + (pass_rank >> 1), 0)
    value = jnp.sum(value.astype(jnp.float32), axis=1, keepdims=True).astype(jnp.int32)
    value = jnp.broadcast_to(value, (32, 128))
    most = jnp.where(place < FIRST, base - 1, base + AHEAD - 1)
    pick[...] = jnp.maximum(jnp.minimum(value, most), 0)


def agree(n_gy, fits, state, verdict, peer, votes, send_sem, recv_sem):
    g, b = lax.axis_index("gx"), lax.axis_index("gy")
    part = g + 1 - 2 * lax.rem(g, 2)
    barrier = pltpu.get_barrier_semaphore()
    pl.semaphore_signal(barrier, inc=1, device_id={"gx": part}, device_id_type=MESH)
    for d in range(1, n_gy):
        pl.semaphore_signal(barrier, inc=1, device_id={"gy": lax.rem(b + d, n_gy)}, device_id_type=MESH)
    votes[0] = fits[...]
    pl.semaphore_wait(barrier, n_gy)
    copies = []
    for d in range(1, n_gy):
        copies.append(pltpu.make_async_remote_copy(
            src_ref=votes.at[0], dst_ref=votes.at[d], send_sem=send_sem.at[d], recv_sem=recv_sem.at[d],
            device_id={"gy": lax.rem(b + d, n_gy)}, device_id_type=MESH,
        ))
    copies.append(pltpu.make_async_remote_copy(
        src_ref=state, dst_ref=peer, send_sem=send_sem.at[0], recv_sem=recv_sem.at[0],
        device_id={"gx": part}, device_id_type=MESH,
    ))
    for copy in copies:
        copy.start()
    for copy in copies:
        copy.wait()
    verdict[0, 0] = jnp.min(jnp.min(votes[...], axis=0))


def routed(
    n_gy, state, peer, w, drive, leak, spot, pick, ldev, lblk, offs, gprev, out, gout,
    own0, own1, own2, own3, gath0, gath1, gath2, gath3,
    headx0, headx1, headx2, headx3, heady0, heady1, heady2, heady3,
    early, late, side, corner, mid, top, bot, wv, dv, gv, acc, xf,
    load_sem, store_sem, local_sem, link_send, link_recv, pass_send, pass_recv, peer_send, peer_recv,
    zsend_sem, zrecv_sem,
):
    seq, units = state.shape[1:]
    rows, cols = w.shape[:2]
    blocks = rows * cols
    nstencil, nlinks = offs.shape[1], ldev.shape[1]
    half = seq // 2
    base = 2 * blocks
    g, b = lax.axis_index("gx"), lax.axis_index("gy")
    core, x, y = lax.rem(g, 2), lax.rem(lax.div(g, 2), 2), lax.div(g, 4)
    part = y * 4 + x * 2 + 1 - core
    along = (y * 4 + (1 - x) * 2 + core, (1 - y) * 4 + x * 2 + core)
    has_left, has_right = b > 0, b < n_gy - 1
    has_up, has_down = g > 0, g < 7
    owns, gaths = (own0, own1, own2, own3), (gath0, gath1, gath2, gath3)
    heads = ((headx0, headx1, headx2, headx3), (heady0, heady1, heady2, heady3))

    def local(src, dst, sem):
        copy = pltpu.make_async_copy(src, dst, sem)
        copy.start()
        return copy

    firsts = []
    for t in (0, 1):
        firsts.append([
            local(state.at[:, pl.ds(t * half, half)], owns[t].at[pl.ds(0, blocks)], load_sem.at[2 * t]),
            local(peer.at[:, pl.ds(t * half, half)], owns[t].at[pl.ds(blocks, blocks)], load_sem.at[2 * t + 1]),
        ])

    barrier = pltpu.get_barrier_semaphore()
    for to in (part, *along):
        pl.semaphore_signal(barrier, inc=1, device_id={"gx": to}, device_id_type=MESH)

    @pl.when(has_left)
    def _():
        pl.semaphore_signal(barrier, inc=1, device_id={"gy": b - 1}, device_id_type=MESH)

    @pl.when(has_right)
    def _():
        pl.semaphore_signal(barrier, inc=1, device_id={"gy": b + 1}, device_id_type=MESH)

    inside = jnp.logical_and(has_left, has_right)

    @pl.when(inside)
    def _():
        pl.semaphore_wait(barrier, 5)

    @pl.when(jnp.logical_not(inside))
    def _():
        pl.semaphore_wait(barrier, 4 if n_gy > 1 else 3)

    bounds = ((0, AHEAD), (AHEAD, FIRST), (FIRST, SLOTS))

    def region(t, link, lead, part_id):
        low, high = bounds[part_id]
        return gaths[t].at[pl.ds(base + 2 * SLOTS * link + (0 if lead else SLOTS) + low, high - low)]

    def link_copy(t, link, part_id):
        low, high = bounds[part_id]
        src = late.at[t, link] if part_id == 2 else early.at[t, link, pl.ds(low, high - low)]
        dst = heads[link][t] if part_id == 0 else region(t, link, True, part_id)
        return pltpu.make_async_remote_copy(
            src_ref=src, dst_ref=dst, send_sem=link_send.at[t, link, part_id], recv_sem=link_recv.at[t, link, part_id],
            device_id={"gx": along[link]}, device_id_type=MESH,
        )

    def pass_copy(t, link, part_id):
        src = heads[link][t] if part_id == 0 else region(t, link, True, part_id)
        return pltpu.make_async_remote_copy(
            src_ref=src, dst_ref=region(t, link, False, part_id),
            send_sem=pass_send.at[t, link, part_id], recv_sem=pass_recv.at[t, link, part_id],
            device_id={"gx": part}, device_id_type=MESH,
        )

    def head_copy(t, link):
        return pltpu.make_async_copy(heads[link][t], region(t, link, True, 0), local_sem.at[t, link])

    def own_copy(t):
        return pltpu.make_async_copy(owns[t], gaths[t].at[pl.ds(0, base)], local_sem.at[t, 2])

    def peer_copy(t, r):
        return pltpu.make_async_remote_copy(
            src_ref=owns[t].at[pl.ds(r * cols, cols)], dst_ref=owns[t].at[pl.ds(blocks + r * cols, cols)],
            send_sem=peer_send.at[t - 2, r], recv_sem=peer_recv.at[t - 2, r],
            device_id={"gx": part}, device_id_type=MESH,
        )

    def rim_copy(t, to, r):
        src = owns[t].at[r * cols + (0 if to == 0 else cols - 1)] if r < rows else corner.at[t, to, r - rows]
        return pltpu.make_async_remote_copy(
            src_ref=src, dst_ref=side.at[t, 1 - to, r],
            send_sem=zsend_sem.at[t, to, r], recv_sem=zrecv_sem.at[t, 1 - to, r],
            device_id={"gy": b - 1 if to == 0 else b + 1}, device_id_type=MESH,
        )

    def rim_wait(t, came, r):
        pltpu.make_async_remote_copy(
            src_ref=side.at[t, came, r], dst_ref=side.at[t, came, r],
            send_sem=zsend_sem.at[t, came, r], recv_sem=zrecv_sem.at[t, came, r],
            device_id={"gy": b - 1 if came == 0 else b + 1}, device_id_type=MESH,
        ).wait_recv()

    def rims(t, do, corners):
        for s, present in ((0, has_left), (1, has_right)):
            for r in ((rows, rows + 1) if corners else range(rows)):
                cond = present
                if corners:
                    cond = jnp.logical_and(present, has_up if r == rows else has_down)

                @pl.when(cond)
                def _():
                    do(t, s, r)

    def begin(t):
        for j in range(FIRST):
            for link in (0, 1):
                early[t, link, j] = owns[t][pick[16 * link + j, 0]]
            if j == AHEAD - 1:
                for link in (0, 1):
                    link_copy(t, link, 0).start()
        for link in (0, 1):
            link_copy(t, link, 1).start()
        rims(t, lambda *at: rim_copy(*at).start(), False)
        own_copy(t).start()

    def follow(t):
        for link in (0, 1):
            link_copy(t, link, 0).wait_recv()
        for link in (0, 1):
            for j in range(LATE):
                at = pick[16 * link + FIRST + j, 0]
                passing = at >= base
                one = owns[t][jnp.where(passing, 0, at)]
                two = heads[1 - link][t][jnp.where(passing, at - base, 0)]
                late[t, link, j] = jnp.where(passing, two, one)
            link_copy(t, link, 2).start()
        for link in (0, 1):
            pass_copy(t, link, 0).start()
            head_copy(t, link).start()

    def relay(t, part_id):
        for link in (0, 1):
            link_copy(t, link, part_id).wait_recv()
            pass_copy(t, link, part_id).start()

    def settle(t):
        own_copy(t).wait()
        for link in (0, 1):
            head_copy(t, link).wait()
            for part_id in range(3):
                pass_copy(t, link, part_id).wait_recv()

    def dot(a, weight):
        return jnp.dot(a, weight, preferred_element_type=jnp.float32)

    def clear():
        zero = jnp.zeros((half, units), jnp.bfloat16)

        @pl.when(jnp.logical_not(has_up))
        def _():
            for c in range(cols + 2):
                top[0, c] = zero

        @pl.when(jnp.logical_not(has_down))
        def _():
            for c in range(cols + 2):
                bot[2, c] = zero

        for at, present in ((0, has_left), (cols + 1, has_right)):

            @pl.when(jnp.logical_not(present))
            def _():
                for r in range(rows):
                    mid[r, at] = zero
                for r in range(3):
                    top[r, at] = zero
                    bot[r, at] = zero

    def put(r, at, value):
        mid[r, at] = value
        if r < 2:
            top[r + 1, at] = value
        if r >= rows - 2:
            bot[r - rows + 2, at] = value

    def fill_mid(t):
        for r in range(rows):
            for c in range(cols):
                put(r, c + 1, owns[t][r * cols + c])
        for s, present in ((0, has_left), (1, has_right)):

            @pl.when(present)
            def _():
                for r in range(rows):
                    put(r, 0 if s == 0 else cols + 1, side[t, s, r])

    def fill_rims(t):
        gath = gaths[t]
        for up, present in ((True, has_up), (False, has_down)):

            @pl.when(present)
            def _():
                for c in range(cols):
                    src = (g - 1) * LANES + (rows - 1) * cols + c if up else (g + 1) * LANES + c
                    value = gath[spot[0, src]]
                    if up:
                        top[0, c + 1] = value
                    else:
                        bot[2, c + 1] = value
                    for to, col in ((0, 0), (1, cols - 1)):
                        if c == col:
                            corner[t, to, 0 if up else 1] = value

    def fill_corners(t):
        for s, has in ((0, has_left), (1, has_right)):
            at = 0 if s == 0 else cols + 1

            @pl.when(jnp.logical_and(has, has_up))
            def _():
                top[0, at] = side[t, s, rows]

            @pl.when(jnp.logical_and(has, has_down))
            def _():
                bot[2, at] = side[t, s, rows + 1]

    def nearby(t, r, near, shift):
        def one(c, carry):
            total = dot(dv[t // 2, r, c, pl.ds(t % 2 * half, half)], wv[r, c, nstencil + nlinks])
            for k in range(nstencil):
                total = total + dot(near[r + shift + offs[0, k], c + 1 + offs[1, k]], wv[r, c, k])
            acc[r * cols + c] = total
            return carry

        lax.fori_loop(0, cols, one, 0)

    def distant(t, r):
        gath = gaths[t]

        def one(c, carry):
            i = r * cols + c
            total = acc[i]
            for l in range(nlinks):
                src = spot[0, ldev[g, l, 0, i] * LANES + lblk[g, l, 0, i]]
                total = total + dot(gath[src], wv[r, c, nstencil + l])
            rate = leak[c, pl.ds(r, 1), :]
            old = owns[t][i].astype(jnp.float32)
            now = ((1.0 - rate) * old + rate * jnp.tanh(total)).astype(jnp.bfloat16)
            if t >= 2:
                xf[i, pl.ds((t - 2) * half, half)] = now
            else:
                owns[t + 2][i] = now
            return carry

        lax.fori_loop(0, cols, one, 0)

    def gram_of(t):
        def one(i, carry):
            now = owns[t + 2][i]
            r, c = i // cols, lax.rem(i, cols)
            gv[r, c] += lax.dot_general(now, now, (((0,), (0,)), ((), ())), preferred_element_type=jnp.float32)
            return carry

        lax.fori_loop(0, blocks, one, 0)

    loads, stores = [], []

    def finished(t, r):
        if t < 2:
            peer_copy(t + 2, r).start()
        if t == 3:
            stores.append(local(xf.at[pl.ds(r * cols, cols)], out.at[r], store_sem.at[1 + r]))

    for copy in firsts[0]:
        copy.wait()
    begin(0)
    for copy in firsts[1]:
        copy.wait()
    for r in range(rows):
        loads.append(local(w.at[r], wv.at[r], load_sem.at[4 + r]))
    loads.append(local(drive, dv, load_sem.at[4 + rows]))
    loads.append(local(gprev, gv, load_sem.at[5 + rows]))
    clear()
    follow(0)
    begin(1)
    for copy in loads:
        copy.wait()
    for t in range(4):
        rims(t, rim_wait, False)
        fill_mid(t)
        for r in range(1, rows - 1):
            nearby(t, r, mid, 0)
        relay(t, 1)
        relay(t, 2)
        settle(t)
        fill_rims(t)
        rims(t, lambda *at: rim_copy(*at).start(), True)
        for r in range(1, rows - 1):
            distant(t, r)
            finished(t, r)
        rims(t, rim_wait, True)
        fill_corners(t)
        for r, near, shift in ((0, top, 1), (rows - 1, bot, 2 - rows)):
            nearby(t, r, near, shift)
            distant(t, r)
            finished(t, r)
        if t < 3:
            follow(t + 1)
        if t < 2:
            for r in range(rows):
                peer_copy(t + 2, r).wait_recv()
            begin(t + 2)
            gram_of(t)
        if t == 1:
            stores.append(local(gv, gout, store_sem.at[0]))
    for t in range(4):
        for link in (0, 1):
            for part_id in range(3):
                link_copy(t, link, part_id).wait_send()
                pass_copy(t, link, part_id).wait_send()
        rims(t, lambda *at: rim_copy(*at).wait_send(), False)
        rims(t, lambda *at: rim_copy(*at).wait_send(), True)
        if t >= 2:
            for r in range(rows):
                peer_copy(t, r).wait_send()
    for copy in stores:
        copy.wait()


def general(n_gy, state, weights, drive, leak, link_dev, link_blk, offsets, gram_prev):
    rows, cols, seq, units = state.shape
    blocks = rows * cols
    anywhere = pl.BlockSpec(memory_space=pl.ANY)
    scalars = pl.BlockSpec(memory_space=pltpu.SMEM)
    block = (seq // 2, units)
    return pl.pallas_call(
        functools.partial(reservoir, n_gy),
        out_shape=(
            jax.ShapeDtypeStruct(state.shape, state.dtype),
            jax.ShapeDtypeStruct(gram_prev.shape, gram_prev.dtype),
        ),
        in_specs=[
            anywhere, anywhere, anywhere, pl.BlockSpec(memory_space=pltpu.VMEM),
            scalars, scalars, scalars, anywhere,
        ],
        out_specs=(anywhere, anywhere),
        scratch_shapes=[
            *[pltpu.VMEM((8, blocks, *block), jnp.bfloat16)] * 4,
            *[pltpu.VMEM((rows + 2, cols + 2, *block), jnp.bfloat16)] * 4,
            pltpu.VMEM(weights.shape, weights.dtype),
            pltpu.VMEM(drive.shape, drive.dtype),
            pltpu.VMEM(gram_prev.shape, gram_prev.dtype),
            pltpu.VMEM((blocks, *block), jnp.float32),
            pltpu.VMEM((blocks, seq, units), jnp.bfloat16),
            pltpu.SemaphoreType.DMA((14,)),
            pltpu.SemaphoreType.DMA((8,)),
            pltpu.SemaphoreType.DMA((112,)),
            pltpu.SemaphoreType.DMA((4, 7, 4)),
            pltpu.SemaphoreType.DMA((4, 2, 6)),
            pltpu.SemaphoreType.DMA((4, 2, 6)),
        ],
        compiler_params=pltpu.CompilerParams(
            collective_id=0, has_side_effects=True, vmem_limit_bytes=62 * 1024 * 1024
        ),
    )(
        state, weights, drive, leak, link_dev, link_blk, offsets, gram_prev,
    )


def finish_gram(last, gram_part):
    rows = last.shape[0]
    state, gram_prev = last, gram_part
    anywhere = pl.BlockSpec(memory_space=pl.ANY)
    return pl.pallas_call(
        closing,
        out_shape=(
            jax.ShapeDtypeStruct(state.shape, state.dtype),
            jax.ShapeDtypeStruct(gram_prev.shape, gram_prev.dtype),
        ),
        in_specs=[anywhere, anywhere],
        out_specs=(anywhere, anywhere),
        scratch_shapes=[
            pltpu.VMEM(state.shape, state.dtype),
            pltpu.VMEM(gram_prev.shape, gram_prev.dtype),
            *[pltpu.SemaphoreType.DMA((rows,))] * 4,
        ],
        compiler_params=pltpu.CompilerParams(vmem_limit_bytes=62 * 1024 * 1024),
    )(last, gram_part)


def listed(n_gy, peer, spot, pick, state, weights, drive, leak, link_dev, link_blk, offsets, gram_prev):
    rows, cols, seq, units = state.shape
    blocks = rows * cols
    anywhere = pl.BlockSpec(memory_space=pl.ANY)
    scalars = pl.BlockSpec(memory_space=pltpu.SMEM)
    block = (seq // 2, units)
    held = lambda *n: pltpu.VMEM((*n, *block), jnp.bfloat16)
    copies = pltpu.SemaphoreType.DMA
    return pl.pallas_call(
        functools.partial(routed, n_gy),
        out_shape=(
            jax.ShapeDtypeStruct(state.shape, state.dtype),
            jax.ShapeDtypeStruct(gram_prev.shape, gram_prev.dtype),
        ),
        in_specs=[
            anywhere, anywhere, anywhere, anywhere, pl.BlockSpec(memory_space=pltpu.VMEM),
            scalars, scalars, scalars, scalars, scalars, anywhere,
        ],
        out_specs=(anywhere, anywhere),
        scratch_shapes=[
            *[held(2 * blocks)] * 4,
            *[held(2 * blocks + 4 * SLOTS)] * 4,
            *[held(AHEAD)] * 8,
            held(4, 2, FIRST), held(4, 2, LATE), held(4, 2, rows + 2), held(4, 2, 2),
            held(rows, cols + 2), held(3, cols + 2), held(3, cols + 2),
            pltpu.VMEM(weights.shape, weights.dtype),
            pltpu.VMEM(drive.shape, drive.dtype),
            pltpu.VMEM(gram_prev.shape, gram_prev.dtype),
            pltpu.VMEM((blocks, *block), jnp.float32),
            pltpu.VMEM((blocks, seq, units), jnp.bfloat16),
            copies((6 + rows,)), copies((1 + rows,)), copies((4, 3)),
            *[copies((4, 2, 3))] * 4,
            *[copies((2, rows))] * 2,
            *[copies((4, 2, rows + 2))] * 2,
        ],
        compiler_params=pltpu.CompilerParams(
            collective_id=2, has_side_effects=True, vmem_limit_bytes=62 * 1024 * 1024
        ),
    )(
        state.reshape(blocks, seq, units), peer, weights, drive, leak, spot, pick,
        link_dev, link_blk, offsets, gram_prev,
    )


def fast_shards(n_gy, state, weights, drive, leak, link_dev, link_blk, offsets, gram_prev):
    rows, cols, seq, units = state.shape
    blocks = rows * cols
    anywhere = pl.BlockSpec(memory_space=pl.ANY)
    vector = pl.BlockSpec(memory_space=pltpu.VMEM)
    scalars = pl.BlockSpec(memory_space=pltpu.SMEM)
    ldev, lblk = link_dev.transpose(0, 3, 1, 2), link_blk.transpose(0, 3, 1, 2)
    table = lambda n: jax.ShapeDtypeStruct((n, 128), jnp.int32)
    spot, pick, fits = pl.pallas_call(
        route, out_shape=(table(8), table(32), table(8)), in_specs=[scalars, scalars], out_specs=(vector,) * 3,
    )(ldev, lblk)
    verdict, peer = pl.pallas_call(
        functools.partial(agree, n_gy),
        out_shape=(
            jax.ShapeDtypeStruct((1, 1), jnp.int32), jax.ShapeDtypeStruct((blocks, seq, units), state.dtype)
        ),
        in_specs=[vector, anywhere],
        out_specs=(scalars, anywhere),
        scratch_shapes=[
            pltpu.VMEM((n_gy, 8, 128), jnp.int32),
            pltpu.SemaphoreType.DMA((n_gy,)),
            pltpu.SemaphoreType.DMA((n_gy,)),
        ],
        compiler_params=pltpu.CompilerParams(collective_id=1, has_side_effects=True),
    )(fits, state.reshape(blocks, seq, units))
    operands = (state, weights, drive, leak.transpose(1, 0, 2), ldev, lblk, offsets.T, gram_prev)
    last, gram = lax.cond(
        verdict.reshape(()) > 0,
        lambda: listed(n_gy, peer, spot, pick, *operands),
        lambda: general(n_gy, *operands),
    )
    return finish_gram(last, gram)


def solution(mesh):
    part = shards
    if mesh.shape["gx"] == 8:
        part = functools.partial(fast_shards, mesh.shape["gy"])
    return jax.shard_map(
        part,
        mesh=mesh,
        in_specs=(
            P("gx", "gy", None, None),
            P("gx", "gy", None, None, None),
            P(None, "gx", "gy", None, None),
            P("gx", "gy", None),
            P(None, "gy", None, None),
            P(None, "gy", None, None),
            P(),
            P("gx", "gy", None, None),
        ),
        out_specs=(P("gx", "gy", None, None), P("gx", "gy", None, None)),
        check_vma=False,
    )
```

```python
import functools

import jax
import jax.numpy as jnp
from jax import lax
from jax.experimental import pallas as pl
from jax.experimental.pallas import tpu as pltpu
from jax.sharding import PartitionSpec as P

MESH = pl.DeviceIdType.MESH
PART, ALONG_X, ALONG_Y, X_PART, Y_PART, DIAG, D_PART = range(7)


def padded(x, sides, width):
    for axis, dim in sides:
        size, length = (lax.axis_size(axis), x.shape[dim])
        up = [(i, (i + 1) % size) for i in range(size - 1)]
        down = [(j, i) for i, j in up]
        last = lax.slice_in_dim(x, length - width, length, axis=dim)
        first = lax.slice_in_dim(x, 0, width, axis=dim)
        before = lax.ppermute(last, axis, up)
        after = lax.ppermute(first, axis, down)
        x = jnp.concatenate([before, x, after], axis=dim)
    return x


def shards(state, weights, drive, leak, link_dev, link_blk, offsets, gram_prev):
    grid_rows, grid_cols, batch_cols, units = state.shape
    nblocks = grid_rows * grid_cols
    nlinks = link_dev.shape[-1]
    nstencil = offsets.shape[0]
    gx_size = lax.axis_size("gx")
    own_index = lax.axis_index("gx")
    all_dev = link_dev[:, 0].reshape(gx_size, nblocks * nlinks)
    all_blk = link_blk[:, 0].reshape(gx_size, nblocks * nlinks)
    my_dev = lax.dynamic_index_in_dim(all_dev, own_index, 0, keepdims=False)
    my_blk = lax.dynamic_index_in_dim(all_blk, own_index, 0, keepdims=False)
    w_long = weights[:, :, nstencil : nstencil + nlinks].reshape(nblocks, nlinks, units, units)
    current = state
    gram = gram_prev
    for step_id in range(drive.shape[0]):
        extended = padded(current, (("gx", 0), ("gy", 1)), 1)
        preact = jnp.zeros((grid_rows, grid_cols, batch_cols, units), jnp.float32)
        for offset_id in range(nstencil):
            zero = jnp.zeros((), jnp.int32)
            start_r = 1 + offsets[offset_id, 0]
            start_c = 1 + offsets[offset_id, 1]
            nearby = lax.dynamic_slice(
                extended, (start_r, start_c, zero, zero), (grid_rows, grid_cols, batch_cols, units)
            )
            preact = preact + jnp.einsum(
                "rcsu,rcuv->rcsv",
                nearby,
                weights[:, :, offset_id],
                preferred_element_type=jnp.float32,
            )
        flat_state = current.reshape(nblocks, batch_cols, units)
        whole = lax.all_gather(flat_state[None], "gx", axis=0, tiled=True)
        picked = whole.reshape(gx_size * nblocks, batch_cols, units)[my_dev * nblocks + my_blk]
        picked = picked.reshape(nblocks, nlinks, batch_cols, units)
        distant = jnp.einsum("blsu,bluv->bsv", picked, w_long, preferred_element_type=jnp.float32)
        preact = preact + distant.reshape(grid_rows, grid_cols, batch_cols, units)
        preact = preact + jnp.einsum(
            "rcsu,rcuv->rcsv",
            drive[step_id],
            weights[:, :, nstencil + nlinks],
            preferred_element_type=jnp.float32,
        )
        rate = leak[:, :, None, :]
        current = ((1.0 - rate) * current.astype(jnp.float32) + rate * jnp.tanh(preact)).astype(
            jnp.bfloat16
        )
        gram = gram + jnp.einsum(
            "rcsu,rcsv->rcuv", current, current, preferred_element_type=jnp.float32
        )
    return (current, gram)


def reservoir(
    n_gy, state, w, drive, leak, ldev, lblk, offs, gprev, out, gout,
    gath00, gath01, gath10, gath11, ext00, ext01, ext10, ext11, wv, dv, gv, acc, xf,
    load_sem, store_sem, send_sem, recv_sem, zsend_sem, zrecv_sem,
):
    rows, cols, seq, units = state.shape
    nstencil, nlinks = offs.shape[1], ldev.shape[1]
    half = seq // 2
    g, b = lax.axis_index("gx"), lax.axis_index("gy")
    core, x, y = lax.rem(g, 2), lax.rem(lax.div(g, 2), 2), lax.div(g, 4)
    near = lambda fy, fx, fc: (
        (1 - y if fy else y) * 4 + (1 - x if fx else x) * 2 + (1 - core if fc else core)
    )
    ids = {
        PART: near(0, 0, 1), ALONG_X: near(0, 1, 0), ALONG_Y: near(1, 0, 0),
        X_PART: near(0, 1, 1), Y_PART: near(1, 0, 1), DIAG: near(1, 1, 0), D_PART: near(1, 1, 1),
    }
    has_left, has_right = b > 0, b < n_gy - 1
    has_up, has_down = g > 0, g < 7
    gaths, exts = (gath00, gath01, gath10, gath11), (ext00, ext01, ext10, ext11)

    loads = []

    def load(src, dst):
        copy = pltpu.make_async_copy(src, dst, load_sem.at[len(loads)])
        copy.start()
        loads.append(copy)
        return copy

    for r in range(rows):
        for s in (0, 1):
            load(state.at[r, :, pl.ds(s * half, half)], gaths[s].at[g, pl.ds(r * cols, cols)])

    barrier = pltpu.get_barrier_semaphore()
    for rel in (PART, ALONG_X, ALONG_Y):
        pl.semaphore_signal(barrier, inc=1, device_id={"gx": ids[rel]}, device_id_type=MESH)

    @pl.when(has_left)
    def _():
        pl.semaphore_signal(barrier, inc=1, device_id={"gy": b - 1}, device_id_type=MESH)

    @pl.when(has_right)
    def _():
        pl.semaphore_signal(barrier, inc=1, device_id={"gy": b + 1}, device_id_type=MESH)

    inside = jnp.logical_and(has_left, has_right)

    @pl.when(inside)
    def _():
        pl.semaphore_wait(barrier, 5)

    @pl.when(jnp.logical_not(inside))
    def _():
        pl.semaphore_wait(barrier, 4 if n_gy > 1 else 3)

    sends = []

    def send(t, rel_from, r, to, rel_there):
        origin = g if rel_from is None else ids[rel_from]
        here = gaths[t].at[origin, pl.ds(r * cols, cols)]
        src = state.at[r, :, pl.ds(t * half, half)] if rel_from is None and t < 2 else here
        copy = pltpu.make_async_remote_copy(
            src_ref=src, dst_ref=here,
            send_sem=send_sem.at[len(sends)], recv_sem=recv_sem.at[t, rel_there, r],
            device_id={"gx": ids[to]}, device_id_type=MESH,
        )
        copy.start()
        sends.append(copy)

    def send_own(t, r, to):
        send(t, None, r, to, to)

    def arrived(t, rel, r):
        here = gaths[t].at[ids[rel], pl.ds(r * cols, cols)]
        pltpu.make_async_remote_copy(
            src_ref=here, dst_ref=here,
            send_sem=send_sem.at[0], recv_sem=recv_sem.at[t, rel, r],
            device_id={"gx": ids[PART]}, device_id_type=MESH,
        ).wait_recv()

    def relay(t, rel, r, across=None):
        arrived(t, rel, r)
        if across is not None:
            send(t, rel, r, across, DIAG)
        send(t, rel, r, PART, {ALONG_X: X_PART, ALONG_Y: Y_PART, DIAG: D_PART}[rel])

    def rim_copy(t, side, kind):
        col = 0 if side == 0 else cols - 1
        there = cols + 1 if side == 0 else 0
        gath, ext = gaths[t], exts[t]
        if kind == 0:
            return [
                pltpu.make_async_remote_copy(
                    src_ref=state.at[r, col, pl.ds(t * half, half)]
                    if t < 2
                    else gath.at[g, r * cols + col],
                    dst_ref=ext.at[r + 1, there],
                    send_sem=zsend_sem.at[t, side, r], recv_sem=zrecv_sem.at[t, side, r],
                    device_id={"gy": b - 1 if side == 0 else b + 1}, device_id_type=MESH,
                )
                for r in range(rows)
            ]
        src = (
            gath.at[lax.rem(g + 7, 8), (rows - 1) * cols + col]
            if kind == 1
            else gath.at[lax.rem(g + 1, 8), col]
        )
        return [
            pltpu.make_async_remote_copy(
                src_ref=src,
                dst_ref=ext.at[0 if kind == 1 else rows + 1, there],
                send_sem=zsend_sem.at[t, side, rows + kind - 1],
                recv_sem=zrecv_sem.at[t, side, rows + kind - 1],
                device_id={"gy": b - 1 if side == 0 else b + 1}, device_id_type=MESH,
            )
        ]

    def rims(t, do, kinds):
        for side in (0, 1):
            present = (has_left, has_right)
            who = present[side] if do != "wait_recv" else present[1 - side]
            for kind in kinds:
                cond = who
                if kind == 1:
                    cond = jnp.logical_and(who, has_up)
                if kind == 2:
                    cond = jnp.logical_and(who, has_down)

                @pl.when(cond)
                def _():
                    for copy in rim_copy(t, side, kind):
                        getattr(copy, do)()

    def begin(t, r):
        if r != 2:
            send_own(t, r, ALONG_X)
        if r != 1:
            send_own(t, r, ALONG_Y)
        send_own(t, r, PART)

    def exchange(t):
        relay(t, ALONG_X, 0, ALONG_Y)
        send_own(t, 1, ALONG_Y)
        relay(t, ALONG_Y, 0)
        relay(t, ALONG_X, 3)
        relay(t, ALONG_Y, 3, ALONG_X)
        send_own(t, 2, ALONG_X)
        relay(t, ALONG_X, 1, ALONG_Y)
        relay(t, ALONG_Y, 2, ALONG_X)

    def borders(t):
        relay(t, DIAG, 0)
        relay(t, DIAG, 3)
        for rel in (PART, X_PART, D_PART):
            arrived(t, rel, 0)
            arrived(t, rel, 3)
        rims(t, "start", (1, 2))
        fill(t)
        rims(t, "wait_recv", (0, 1, 2))

    def finish(t):
        relay(t, ALONG_Y, 1)
        relay(t, ALONG_X, 2)
        relay(t, DIAG, 1)
        relay(t, DIAG, 2)
        for rel in (PART, X_PART, D_PART):
            arrived(t, rel, 1)
            arrived(t, rel, 2)
        for r in range(rows):
            arrived(t, Y_PART, r)

    def fill(t):
        gath, ext = gaths[t], exts[t]

        def place(i, carry):
            r, c = i // cols, lax.rem(i, cols)
            ext[r + 1, c + 1] = gath[g, i]
            return carry

        lax.fori_loop(0, rows * cols, place, 0)
        zero = jnp.zeros((half, units), jnp.bfloat16)

        @pl.when(has_up)
        def _():
            for c in range(cols):
                ext[0, c + 1] = gath[lax.rem(g + 7, 8), (rows - 1) * cols + c]

        @pl.when(has_down)
        def _():
            for c in range(cols):
                ext[rows + 1, c + 1] = gath[lax.rem(g + 1, 8), c]

        for there, edge in ((0, has_up), (rows + 1, has_down)):

            @pl.when(jnp.logical_not(edge))
            def _():
                for c in range(cols + 2):
                    ext[there, c] = zero

        for there, side in ((0, has_left), (cols + 1, has_right)):

            @pl.when(jnp.logical_not(side))
            def _():
                for r in range(rows):
                    ext[r + 1, there] = zero
                for r, edge in ((0, has_up), (rows + 1, has_down)):

                    @pl.when(edge)
                    def _():
                        ext[r, there] = zero

    def dot(a, weight):
        return jnp.dot(a, weight, preferred_element_type=jnp.float32)

    def nearby(t):
        ext = exts[t]

        def one(i, carry):
            r, c = i // cols, lax.rem(i, cols)
            total = dot(
                dv[t // 2, r, c, pl.ds(t % 2 * half, half)], wv[r, c, nstencil + nlinks]
            )
            for k in range(nstencil):
                total = total + dot(ext[r + 1 + offs[0, k], c + 1 + offs[1, k]], wv[r, c, k])
            acc[i] = total
            return carry

        lax.fori_loop(0, rows * cols, one, 0)

    def gram_of(r, c, now):
        gv[r, c] += lax.dot_general(
            now, now, (((0,), (0,)), ((), ())), preferred_element_type=jnp.float32
        )

    def distant(t, r):
        gath = gaths[t]

        def one(c, carry):
            i = r * cols + c
            total = acc[i]
            for l in range(nlinks):
                total = total + dot(gath[ldev[g, l, 0, i], lblk[g, l, 0, i]], wv[r, c, nstencil + l])
            rate = leak[c, pl.ds(r, 1), :]
            old = gath[g, i].astype(jnp.float32)
            now = ((1.0 - rate) * old + rate * jnp.tanh(total)).astype(jnp.bfloat16)
            if t >= 2:
                xf[i, pl.ds((t - 2) * half, half)] = now
            else:
                gaths[t + 2][g, i] = now
            if t < 3:
                gram_of(r, c, now)
            return carry

        lax.fori_loop(0, cols, one, 0)

    order = (0, 3, 1, 2)

    def start(t):
        for r in order:
            begin(t, r)
        rims(t, "start", (0,))

    stores = []

    def store(src, dst):
        copy = pltpu.make_async_copy(src, dst, store_sem.at[len(stores)])
        copy.start()
        stores.append(copy)

    start(0)
    for r in range(rows):
        load(w.at[r], wv.at[r])
    load(drive, dv)
    load(gprev, gv)
    for t in range(4):
        exchange(t)
        if t < 3:
            start(t + 1)
        if t == 0:
            for copy in loads:
                copy.wait()
        borders(t)
        nearby(t)
        finish(t)
        for r in range(rows):
            distant(t, r)
            if t == 3:
                store(xf.at[pl.ds(r * cols, cols)], out.at[r])
        if t == 2:
            store(gv, gout)
    for copy in sends:
        copy.wait_send()
    for t in range(4):
        rims(t, "wait_send", (0, 1, 2))
    for copy in stores:
        copy.wait()


def closing(half, x, gram, out, gout, xv, gv, x_sem, g_sem, out_sem, gout_sem):
    rows, cols = x.shape[:2]
    copy = pltpu.make_async_copy
    x_in = [copy(x.at[r], xv.at[r], x_sem.at[r]) for r in range(rows)]
    g_in = [copy(gram.at[r], gv.at[r], g_sem.at[r]) for r in range(rows)]
    x_out = [copy(xv.at[r], out.at[r], out_sem.at[r]) for r in range(rows)]
    g_out = [copy(gv.at[r], gout.at[r], gout_sem.at[r]) for r in range(rows)]
    for r in range(rows):
        x_in[r].start()
        g_in[r].start()
    for r in range(rows):
        x_in[r].wait()
        x_out[r].start()
        g_in[r].wait()
        for c in range(cols):
            now = xv[r, c, pl.ds(half, half)]
            gv[r, c] += lax.dot_general(
                now, now, (((0,), (0,)), ((), ())), preferred_element_type=jnp.float32
            )
        g_out[r].start()
    for r in range(rows):
        x_out[r].wait()
        g_out[r].wait()


SLOTS, FIRST, AHEAD = 13, 8, 5
LATE = SLOTS - FIRST
LANES = 16


def route(ldev, lblk, spot, pick):
    rows_of = lambda n: lax.broadcasted_iota(jnp.int32, (n, 128), 0)
    lanes_of = lambda n: lax.broadcasted_iota(jnp.int32, (n, 128), 1)
    nlinks, nblocks = ldev.shape[1], ldev.shape[3]
    g = lax.axis_index("gx")
    core, home = g % 2, g // 2
    lane = lanes_of(8)
    chip, block = lane // 32, lane % LANES

    needs = []
    for c in range(4):
        need = jnp.zeros((8, 128), jnp.bool_)
        for a in (2 * c, 2 * c + 1):
            for l in range(nlinks):
                for q in range(nblocks):
                    need = need | (lane == ldev[a, l, 0, q] * LANES + lblk[a, l, 0, q])
        for src, dst in ((2 * c - 1, 2 * c), (2 * c + 2, 2 * c + 1)):
            if 0 <= src < 8:
                first = nblocks - 3 if src < dst else 0
                need = need | ((lane >= src * LANES + first) & (lane < src * LANES + first + 3))
        needs.append(need.astype(jnp.int32))

    def seen(flip):
        return jnp.where(
            chip == 0, needs[flip],
            jnp.where(chip == 1, needs[1 ^ flip], jnp.where(chip == 2, needs[2 ^ flip], needs[3 ^ flip])),
        )

    nx, ny, nd = seen(1), seen(2), seen(3)
    only_x, both, neither, only_y = nd * nx * (1 - ny), nd * nx * ny, nd * (1 - nx) * (1 - ny), nd * ny * (1 - nx)
    classes = [only_x, both, neither, only_y, nx, ny]

    def stack(parts):
        sub, stacked = rows_of(8), jnp.zeros((8, 128), jnp.int32)
        for k, part in enumerate(parts):
            stacked = jnp.where(sub == k, part, stacked)
        return stacked.astype(jnp.float32)

    def times(x, matrix):
        return jnp.dot(
            x.astype(jnp.bfloat16), matrix.astype(jnp.float32).astype(jnp.bfloat16),
            preferred_element_type=jnp.float32,
        ).astype(jnp.int32)

    above, across = rows_of(128), lanes_of(128)
    upto = (above <= across) & (above // 32 == across // 32)
    counted = stack(classes)
    sums = times(counted, upto)
    totals = [times(counted, above // 32 == c) for c in range(4)]
    row = lambda x, k: jnp.broadcast_to(x[k : k + 1], (8, 128))

    cand = rows_of(32) * 128 + lanes_of(32)
    wide = lambda c, k: jnp.broadcast_to(totals[c][k : k + 1], (32, 128))
    fx, fy, rx, ry = [], [], [], []

    def passed(counts, digit):
        total = counts[0] + counts[1] + counts[2] + counts[3]
        start = (2 * counts[0] + counts[1] + counts[2] + 1) // 2 - 4
        return total, jnp.maximum(jnp.minimum(start + digit, total), 0)

    for c in range(4):
        counts = [wide(c, k) for k in range(6)]
        total, m = passed(counts, (cand >> (3 * c)) & 7)
        rest = total - m
        rx.append(m)
        ry.append(rest)
        fx.append(counts[4] + jnp.maximum(m - counts[0] - counts[1], 0))
        fy.append(
            counts[5] + jnp.maximum(jnp.minimum(rest - counts[3], counts[2]), 0)
            + jnp.maximum(rest - counts[3] - counts[2] - counts[1], 0)
        )
    worst = jnp.zeros((32, 128), jnp.int32)
    for c in range(4):
        worst = jnp.maximum(worst, jnp.maximum(fx[c], 2 * FIRST) + ry[c ^ 2])
        worst = jnp.maximum(worst, jnp.maximum(fy[c], 2 * FIRST) + rx[c ^ 1])
        worst = jnp.where(jnp.maximum(rx[c], ry[c]) > 2 * AHEAD, 255, worst)
    best = jnp.min(worst * 4096 + cand)

    pickc = lambda values: jnp.where(
        chip == 0, values[0], jnp.where(chip == 1, values[1], jnp.where(chip == 2, values[2], values[3]))
    )
    count = [pickc([row(totals[c], k) for c in range(4)]) for k in range(6)]
    digit = pickc([(best >> (3 * c)) & 7 for c in range(4)])
    total, m = passed(count, digit)
    rank = jnp.where(
        only_x > 0, row(sums, 0) - 1,
        jnp.where(
            both > 0, count[0] + row(sums, 1) - 1,
            jnp.where(
                neither > 0, count[0] + count[1] + row(sums, 2) - 1,
                count[0] + count[1] + count[2] + row(sums, 3) - 1,
            ),
        ),
    )
    via_x = jnp.where(rank < m, nd, 0)
    via_y = nd - via_x
    more = times(stack([nx * (1 - via_x), ny * (1 - via_y)]), upto)
    over = rank - m
    pos_x = jnp.where(via_x > 0, rank, m + row(more, 0) - 1)
    pos_y = jnp.where(via_y > 0, over, total - m + row(more, 1) - 1)
    held_x, held_y = jnp.maximum(nx, via_x), jnp.maximum(ny, via_y)

    mine = block + jnp.where((lane // LANES) % 2 == core, 0, 12)
    base = 2 * nblocks
    inward = lambda link, k, p: base + 2 * SLOTS * link + jnp.where(k == core, 0, SLOTS) + p
    odd = lambda x: x & 1
    there = jnp.where(
        chip == home, mine,
        jnp.where(
            chip == (home ^ 1), inward(0, odd(pos_x), pos_x >> 1),
            jnp.where(
                chip == (home ^ 2), inward(1, odd(pos_y + 1), pos_y >> 1),
                jnp.where(
                    via_x > 0, inward(1, odd(rank), SLOTS - 1 - (rank >> 1)),
                    inward(0, odd(over + 1), SLOTS - 1 - (over >> 1)),
                ),
            ),
        ),
    )
    spot[...] = jnp.maximum(jnp.minimum(there, base + 4 * SLOTS - 1), 0)

    sub = rows_of(32)
    place, is_y = sub % 16, sub >= 16
    full = lambda x: jnp.broadcast_to(x[0:1], (32, 128))
    own_chip = full(jnp.where(chip == home, 1, 0)) > 0
    own_at = jnp.where(is_y, full(pos_y), full(pos_x))
    own_core = jnp.where(is_y, odd(own_at + 1), odd(own_at))
    own_held = jnp.where(is_y, full(held_y), full(held_x)) > 0
    own_hit = own_chip & own_held & (own_at >> 1 == place) & (own_core == core)
    pass_x = full(jnp.where(chip == (home ^ 2), via_y, 0))
    pass_y = full(jnp.where(chip == (home ^ 1), via_x, 0))
    pass_held = jnp.where(is_y, pass_y, pass_x) > 0
    pass_rank = jnp.where(is_y, full(rank), full(over))
    pass_core = jnp.where(is_y, odd(pass_rank), odd(pass_rank + 1))
    pass_hit = pass_held & (SLOTS - 1 - (pass_rank >> 1) == place) & (pass_core == core)
    value = jnp.where(own_hit, full(mine), 0) + jnp.where(pass_hit, base + (pass_rank >> 1), 0)
    value = jnp.sum(value.astype(jnp.float32), axis=1, keepdims=True).astype(jnp.int32)
    value = jnp.broadcast_to(value, (32, 128))
    most = jnp.where(place < FIRST, base - 1, base + AHEAD - 1)
    pick[...] = jnp.maximum(jnp.minimum(value, most), 0)
    return jnp.where(jnp.zeros((8, 128), jnp.int32) + (best >> 12) <= 2 * SLOTS, 1, 0)


def agree(n_gy, ldev, lblk, state, spot, pick, verdict, peer, votes, send_sem, recv_sem):
    g, b = lax.axis_index("gx"), lax.axis_index("gy")
    part = g + 1 - 2 * lax.rem(g, 2)
    barrier = pltpu.get_barrier_semaphore()
    pl.semaphore_signal(barrier, inc=1, device_id={"gx": part}, device_id_type=MESH)
    for d in range(1, n_gy):
        pl.semaphore_signal(barrier, inc=1, device_id={"gy": lax.rem(b + d, n_gy)}, device_id_type=MESH)
    votes[0] = route(ldev, lblk, spot, pick)
    pl.semaphore_wait(barrier, n_gy)
    copies = []
    for d in range(1, n_gy):
        copies.append(pltpu.make_async_remote_copy(
            src_ref=votes.at[0], dst_ref=votes.at[d], send_sem=send_sem.at[d], recv_sem=recv_sem.at[d],
            device_id={"gy": lax.rem(b + d, n_gy)}, device_id_type=MESH,
        ))
    copies.append(pltpu.make_async_remote_copy(
        src_ref=state, dst_ref=peer, send_sem=send_sem.at[0], recv_sem=recv_sem.at[0],
        device_id={"gx": part}, device_id_type=MESH,
    ))
    for copy in copies:
        copy.start()
    for copy in copies:
        copy.wait()
    verdict[0, 0] = jnp.min(jnp.min(votes[...], axis=0))


def routed(
    n_gy, state, peer, w, drive, leak, spot, pick, ldev, lblk, offs, gprev, out, gout,
    own0, own1, own2, own3, gath0, gath1, gath2, gath3,
    headx0, headx1, headx2, headx3, heady0, heady1, heady2, heady3,
    early, late, side, corner, mid, top, bot, wv, dv, gv, acc, xf,
    load_sem, store_sem, local_sem, link_send, link_recv, pass_send, pass_recv, peer_send, peer_recv,
    zsend_sem, zrecv_sem,
):
    seq, units = state.shape[1:]
    rows, cols = w.shape[:2]
    blocks = rows * cols
    nstencil, nlinks = offs.shape[1], ldev.shape[1]
    half = seq // 2
    base = 2 * blocks
    g, b = lax.axis_index("gx"), lax.axis_index("gy")
    core, x, y = lax.rem(g, 2), lax.rem(lax.div(g, 2), 2), lax.div(g, 4)
    part = y * 4 + x * 2 + 1 - core
    along = (y * 4 + (1 - x) * 2 + core, (1 - y) * 4 + x * 2 + core)
    has_left, has_right = b > 0, b < n_gy - 1
    has_up, has_down = g > 0, g < 7
    owns, gaths = (own0, own1, own2, own3), (gath0, gath1, gath2, gath3)
    heads = ((headx0, headx1, headx2, headx3), (heady0, heady1, heady2, heady3))

    def local(src, dst, sem):
        copy = pltpu.make_async_copy(src, dst, sem)
        copy.start()
        return copy

    firsts = []
    for t in (0, 1):
        firsts.append([
            local(state.at[:, pl.ds(t * half, half)], owns[t].at[pl.ds(0, blocks)], load_sem.at[2 * t]),
            local(peer.at[:, pl.ds(t * half, half)], owns[t].at[pl.ds(blocks, blocks)], load_sem.at[2 * t + 1]),
        ])

    barrier = pltpu.get_barrier_semaphore()
    for to in (part, *along):
        pl.semaphore_signal(barrier, inc=1, device_id={"gx": to}, device_id_type=MESH)

    @pl.when(has_left)
    def _():
        pl.semaphore_signal(barrier, inc=1, device_id={"gy": b - 1}, device_id_type=MESH)

    @pl.when(has_right)
    def _():
        pl.semaphore_signal(barrier, inc=1, device_id={"gy": b + 1}, device_id_type=MESH)

    inside = jnp.logical_and(has_left, has_right)

    @pl.when(inside)
    def _():
        pl.semaphore_wait(barrier, 5)

    @pl.when(jnp.logical_not(inside))
    def _():
        pl.semaphore_wait(barrier, 4 if n_gy > 1 else 3)

    bounds = ((0, AHEAD), (AHEAD, FIRST), (FIRST, SLOTS))

    def region(t, link, lead, part_id):
        low, high = bounds[part_id]
        return gaths[t].at[pl.ds(base + 2 * SLOTS * link + (0 if lead else SLOTS) + low, high - low)]

    def link_copy(t, link, part_id):
        low, high = bounds[part_id]
        src = late.at[t, link] if part_id == 2 else early.at[t, link, pl.ds(low, high - low)]
        dst = heads[link][t] if part_id == 0 else region(t, link, True, part_id)
        return pltpu.make_async_remote_copy(
            src_ref=src, dst_ref=dst, send_sem=link_send.at[t, link, part_id], recv_sem=link_recv.at[t, link, part_id],
            device_id={"gx": along[link]}, device_id_type=MESH,
        )

    def pass_copy(t, link, part_id):
        src = heads[link][t] if part_id == 0 else region(t, link, True, part_id)
        return pltpu.make_async_remote_copy(
            src_ref=src, dst_ref=region(t, link, False, part_id),
            send_sem=pass_send.at[t, link, part_id], recv_sem=pass_recv.at[t, link, part_id],
            device_id={"gx": part}, device_id_type=MESH,
        )

    def head_copy(t, link):
        return pltpu.make_async_copy(heads[link][t], region(t, link, True, 0), local_sem.at[t, link])

    def own_copy(t):
        return pltpu.make_async_copy(owns[t], gaths[t].at[pl.ds(0, base)], local_sem.at[t, 2])

    def peer_copy(t, r):
        return pltpu.make_async_remote_copy(
            src_ref=owns[t].at[pl.ds(r * cols, cols)], dst_ref=owns[t].at[pl.ds(blocks + r * cols, cols)],
            send_sem=peer_send.at[t - 2, r], recv_sem=peer_recv.at[t - 2, r],
            device_id={"gx": part}, device_id_type=MESH,
        )

    def rim_copy(t, to, r):
        src = owns[t].at[r * cols + (0 if to == 0 else cols - 1)] if r < rows else corner.at[t, to, r - rows]
        return pltpu.make_async_remote_copy(
            src_ref=src, dst_ref=side.at[t, 1 - to, r],
            send_sem=zsend_sem.at[t, to, r], recv_sem=zrecv_sem.at[t, 1 - to, r],
            device_id={"gy": b - 1 if to == 0 else b + 1}, device_id_type=MESH,
        )

    def rim_wait(t, came, r):
        pltpu.make_async_remote_copy(
            src_ref=side.at[t, came, r], dst_ref=side.at[t, came, r],
            send_sem=zsend_sem.at[t, came, r], recv_sem=zrecv_sem.at[t, came, r],
            device_id={"gy": b - 1 if came == 0 else b + 1}, device_id_type=MESH,
        ).wait_recv()

    def rims(t, do, corners):
        for s, present in ((0, has_left), (1, has_right)):
            for r in ((rows, rows + 1) if corners else range(rows)):
                cond = present
                if corners:
                    cond = jnp.logical_and(present, has_up if r == rows else has_down)

                @pl.when(cond)
                def _():
                    do(t, s, r)

    def begin(t):
        for j in range(FIRST):
            for link in (0, 1):
                early[t, link, j] = owns[t][pick[16 * link + j, 0]]
            if j == AHEAD - 1:
                for link in (0, 1):
                    link_copy(t, link, 0).start()
        for link in (0, 1):
            link_copy(t, link, 1).start()
        rims(t, lambda *at: rim_copy(*at).start(), False)
        own_copy(t).start()

    def follow(t):
        for link in (0, 1):
            link_copy(t, link, 0).wait_recv()
        for link in (0, 1):
            for j in range(LATE):
                at = pick[16 * link + FIRST + j, 0]
                passing = at >= base
                one = owns[t][jnp.where(passing, 0, at)]
                two = heads[1 - link][t][jnp.where(passing, at - base, 0)]
                late[t, link, j] = jnp.where(passing, two, one)
            link_copy(t, link, 2).start()
        for link in (0, 1):
            pass_copy(t, link, 0).start()
            head_copy(t, link).start()

    def relay(t, part_id):
        for link in (0, 1):
            link_copy(t, link, part_id).wait_recv()
            pass_copy(t, link, part_id).start()

    def settle(t):
        own_copy(t).wait()
        for link in (0, 1):
            head_copy(t, link).wait()
            for part_id in range(3):
                pass_copy(t, link, part_id).wait_recv()

    def dot(a, weight):
        return jnp.dot(a, weight, preferred_element_type=jnp.float32)

    def clear():
        zero = jnp.zeros((half, units), jnp.bfloat16)

        @pl.when(jnp.logical_not(has_up))
        def _():
            for c in range(cols + 2):
                top[0, c] = zero

        @pl.when(jnp.logical_not(has_down))
        def _():
            for c in range(cols + 2):
                bot[2, c] = zero

        for at, present in ((0, has_left), (cols + 1, has_right)):

            @pl.when(jnp.logical_not(present))
            def _():
                for r in range(rows):
                    mid[r, at] = zero
                for r in range(3):
                    top[r, at] = zero
                    bot[r, at] = zero

    def put(r, at, value):
        mid[r, at] = value
        if r < 2:
            top[r + 1, at] = value
        if r >= rows - 2:
            bot[r - rows + 2, at] = value

    def fill_mid(t):
        for r in range(rows):
            for c in range(cols):
                put(r, c + 1, owns[t][r * cols + c])
        for s, present in ((0, has_left), (1, has_right)):

            @pl.when(present)
            def _():
                for r in range(rows):
                    put(r, 0 if s == 0 else cols + 1, side[t, s, r])

    def fill_rims(t):
        gath = gaths[t]
        for up, present in ((True, has_up), (False, has_down)):

            @pl.when(present)
            def _():
                for c in range(cols):
                    src = (g - 1) * LANES + (rows - 1) * cols + c if up else (g + 1) * LANES + c
                    value = gath[spot[0, src]]
                    if up:
                        top[0, c + 1] = value
                    else:
                        bot[2, c + 1] = value
                    for to, col in ((0, 0), (1, cols - 1)):
                        if c == col:
                            corner[t, to, 0 if up else 1] = value

    def fill_corners(t):
        for s, has in ((0, has_left), (1, has_right)):
            at = 0 if s == 0 else cols + 1

            @pl.when(jnp.logical_and(has, has_up))
            def _():
                top[0, at] = side[t, s, rows]

            @pl.when(jnp.logical_and(has, has_down))
            def _():
                bot[2, at] = side[t, s, rows + 1]

    def over(r, body):
        def one(c, carry):
            body(c, r * cols + c)
            return carry

        lax.fori_loop(0, cols, one, 0)

    def driven(t, r, c):
        return dot(dv[t // 2, r, c, pl.ds(t % 2 * half, half)], wv[r, c, nstencil + nlinks])

    def nearby(total, r, c, near, shift):
        for k in range(nstencil):
            total = total + dot(near[r + shift + offs[0, k], c + 1 + offs[1, k]], wv[r, c, k])
        return total

    def distant(total, t, r, c):
        i = r * cols + c
        for l in range(nlinks):
            src = spot[0, ldev[g, l, 0, i] * LANES + lblk[g, l, 0, i]]
            total = total + dot(gaths[t][src], wv[r, c, nstencil + l])
        return total

    def renew(total, t, r, c):
        i = r * cols + c
        rate = leak[c, pl.ds(r, 1), :]
        old = owns[t][i].astype(jnp.float32)
        now = ((1.0 - rate) * old + rate * jnp.tanh(total)).astype(jnp.bfloat16)
        if t >= 2:
            xf[i, pl.ds((t - 2) * half, half)] = now
        else:
            owns[t + 2][i] = now

    def keep(i, total):
        acc[i] = total

    def gram_of(t):
        def one(i, carry):
            now = owns[t + 2][i] if t < 2 else xf[i, pl.ds(0, half)]
            r, c = i // cols, lax.rem(i, cols)
            gv[r, c] += lax.dot_general(now, now, (((0,), (0,)), ((), ())), preferred_element_type=jnp.float32)
            return carry

        lax.fori_loop(0, blocks, one, 0)

    loads, stores = [], []

    def finished(t, r):
        if t < 2:
            peer_copy(t + 2, r).start()
        if t == 3:
            stores.append(local(xf.at[pl.ds(r * cols, cols)], out.at[r], store_sem.at[1 + r]))

    for copy in firsts[0]:
        copy.wait()
    begin(0)
    for copy in firsts[1]:
        copy.wait()
    for r in range(rows):
        loads.append(local(w.at[r], wv.at[r], load_sem.at[4 + r]))
    loads.append(local(drive, dv, load_sem.at[4 + rows]))
    loads.append(local(gprev, gv, load_sem.at[5 + rows]))
    clear()
    follow(0)
    begin(1)
    for copy in loads:
        copy.wait()
    inner, outer = range(1, rows - 1), ((0, top, 1), (rows - 1, bot, 2 - rows))
    for t in range(4):
        rims(t, rim_wait, False)
        fill_mid(t)
        for r in inner:
            over(r, lambda c, i: keep(i, nearby(driven(t, r, c), r, c, mid, 0)))
        for r, _, _ in outer:
            over(r, lambda c, i: keep(i, driven(t, r, c)))
        relay(t, 1)
        relay(t, 2)
        settle(t)
        fill_rims(t)
        rims(t, lambda *at: rim_copy(*at).start(), True)
        for r in inner:
            over(r, lambda c, i: renew(distant(acc[i], t, r, c), t, r, c))
            finished(t, r)
        for r, _, _ in outer:
            over(r, lambda c, i: keep(i, distant(acc[i], t, r, c)))
        if t < 3:
            follow(t + 1)
        rims(t, rim_wait, True)
        fill_corners(t)
        for r, near, shift in outer:
            over(r, lambda c, i: renew(nearby(acc[i], r, c, near, shift), t, r, c))
            finished(t, r)
        if t < 2:
            for r in range(rows):
                peer_copy(t + 2, r).wait_recv()
            begin(t + 2)
        if t < 3:
            gram_of(t)
        if t == 2:
            stores.append(local(gv, gout, store_sem.at[0]))
    for t in range(4):
        for link in (0, 1):
            for part_id in range(3):
                link_copy(t, link, part_id).wait_send()
                pass_copy(t, link, part_id).wait_send()
        rims(t, lambda *at: rim_copy(*at).wait_send(), False)
        rims(t, lambda *at: rim_copy(*at).wait_send(), True)
        if t >= 2:
            for r in range(rows):
                peer_copy(t, r).wait_send()
    for copy in stores:
        copy.wait()


def general(n_gy, state, weights, drive, leak, link_dev, link_blk, offsets, gram_prev):
    rows, cols, seq, units = state.shape
    blocks = rows * cols
    anywhere = pl.BlockSpec(memory_space=pl.ANY)
    scalars = pl.BlockSpec(memory_space=pltpu.SMEM)
    block = (seq // 2, units)
    return pl.pallas_call(
        functools.partial(reservoir, n_gy),
        out_shape=(
            jax.ShapeDtypeStruct(state.shape, state.dtype),
            jax.ShapeDtypeStruct(gram_prev.shape, gram_prev.dtype),
        ),
        in_specs=[
            anywhere, anywhere, anywhere, pl.BlockSpec(memory_space=pltpu.VMEM),
            scalars, scalars, scalars, anywhere,
        ],
        out_specs=(anywhere, anywhere),
        scratch_shapes=[
            *[pltpu.VMEM((8, blocks, *block), jnp.bfloat16)] * 4,
            *[pltpu.VMEM((rows + 2, cols + 2, *block), jnp.bfloat16)] * 4,
            pltpu.VMEM(weights.shape, weights.dtype),
            pltpu.VMEM(drive.shape, drive.dtype),
            pltpu.VMEM(gram_prev.shape, gram_prev.dtype),
            pltpu.VMEM((blocks, *block), jnp.float32),
            pltpu.VMEM((blocks, seq, units), jnp.bfloat16),
            pltpu.SemaphoreType.DMA((14,)),
            pltpu.SemaphoreType.DMA((8,)),
            pltpu.SemaphoreType.DMA((112,)),
            pltpu.SemaphoreType.DMA((4, 7, 4)),
            pltpu.SemaphoreType.DMA((4, 2, 6)),
            pltpu.SemaphoreType.DMA((4, 2, 6)),
        ],
        compiler_params=pltpu.CompilerParams(
            collective_id=0, has_side_effects=True, vmem_limit_bytes=62 * 1024 * 1024
        ),
    )(
        state, weights, drive, leak, link_dev, link_blk, offsets, gram_prev,
    )


def finish_gram(last, gram_part):
    rows = last.shape[0]
    state, gram_prev = last, gram_part
    anywhere = pl.BlockSpec(memory_space=pl.ANY)
    return pl.pallas_call(
        functools.partial(closing, last.shape[2] // 2),
        out_shape=(
            jax.ShapeDtypeStruct(state.shape, state.dtype),
            jax.ShapeDtypeStruct(gram_prev.shape, gram_prev.dtype),
        ),
        in_specs=[anywhere, anywhere],
        out_specs=(anywhere, anywhere),
        scratch_shapes=[
            pltpu.VMEM(state.shape, state.dtype),
            pltpu.VMEM(gram_prev.shape, gram_prev.dtype),
            *[pltpu.SemaphoreType.DMA((rows,))] * 4,
        ],
        compiler_params=pltpu.CompilerParams(vmem_limit_bytes=62 * 1024 * 1024),
    )(last, gram_part)


def listed(n_gy, peer, spot, pick, state, weights, drive, leak, link_dev, link_blk, offsets, gram_prev):
    rows, cols, seq, units = state.shape
    blocks = rows * cols
    anywhere = pl.BlockSpec(memory_space=pl.ANY)
    scalars = pl.BlockSpec(memory_space=pltpu.SMEM)
    block = (seq // 2, units)
    held = lambda *n: pltpu.VMEM((*n, *block), jnp.bfloat16)
    copies = pltpu.SemaphoreType.DMA
    return pl.pallas_call(
        functools.partial(routed, n_gy),
        out_shape=(
            jax.ShapeDtypeStruct(state.shape, state.dtype),
            jax.ShapeDtypeStruct(gram_prev.shape, gram_prev.dtype),
        ),
        in_specs=[
            anywhere, anywhere, anywhere, anywhere, pl.BlockSpec(memory_space=pltpu.VMEM),
            scalars, scalars, scalars, scalars, scalars, anywhere,
        ],
        out_specs=(anywhere, anywhere),
        scratch_shapes=[
            *[held(2 * blocks)] * 4,
            *[held(2 * blocks + 4 * SLOTS)] * 4,
            *[held(AHEAD)] * 8,
            held(4, 2, FIRST), held(4, 2, LATE), held(4, 2, rows + 2), held(4, 2, 2),
            held(rows, cols + 2), held(3, cols + 2), held(3, cols + 2),
            pltpu.VMEM(weights.shape, weights.dtype),
            pltpu.VMEM(drive.shape, drive.dtype),
            pltpu.VMEM(gram_prev.shape, gram_prev.dtype),
            pltpu.VMEM((blocks, *block), jnp.float32),
            pltpu.VMEM((blocks, seq, units), jnp.bfloat16),
            copies((6 + rows,)), copies((1 + rows,)), copies((4, 3)),
            *[copies((4, 2, 3))] * 4,
            *[copies((2, rows))] * 2,
            *[copies((4, 2, rows + 2))] * 2,
        ],
        compiler_params=pltpu.CompilerParams(
            collective_id=2, has_side_effects=True, vmem_limit_bytes=62 * 1024 * 1024
        ),
    )(
        state.reshape(blocks, seq, units), peer, weights, drive, leak, spot, pick,
        link_dev, link_blk, offsets, gram_prev,
    )


def fast_shards(n_gy, state, weights, drive, leak, link_dev, link_blk, offsets, gram_prev):
    rows, cols, seq, units = state.shape
    blocks = rows * cols
    anywhere = pl.BlockSpec(memory_space=pl.ANY)
    vector = pl.BlockSpec(memory_space=pltpu.VMEM)
    scalars = pl.BlockSpec(memory_space=pltpu.SMEM)
    ldev, lblk = link_dev.transpose(0, 3, 1, 2), link_blk.transpose(0, 3, 1, 2)
    table = lambda n: jax.ShapeDtypeStruct((n, 128), jnp.int32)
    spot, pick, verdict, peer = pl.pallas_call(
        functools.partial(agree, n_gy),
        out_shape=(
            table(8), table(32), jax.ShapeDtypeStruct((1, 1), jnp.int32),
            jax.ShapeDtypeStruct((blocks, seq, units), state.dtype),
        ),
        in_specs=[scalars, scalars, anywhere],
        out_specs=(vector, vector, scalars, anywhere),
        scratch_shapes=[
            pltpu.VMEM((n_gy, 8, 128), jnp.int32),
            pltpu.SemaphoreType.DMA((n_gy,)),
            pltpu.SemaphoreType.DMA((n_gy,)),
        ],
        compiler_params=pltpu.CompilerParams(collective_id=1, has_side_effects=True),
    )(ldev, lblk, state.reshape(blocks, seq, units))
    operands = (state, weights, drive, leak.transpose(1, 0, 2), ldev, lblk, offsets.T, gram_prev)
    last, gram = lax.cond(
        verdict.reshape(()) > 0,
        lambda: listed(n_gy, peer, spot, pick, *operands),
        lambda: general(n_gy, *operands),
    )
    return finish_gram(last, gram)


def solution(mesh):
    part = shards
    if mesh.shape["gx"] == 8:
        part = functools.partial(fast_shards, mesh.shape["gy"])
    return jax.shard_map(
        part,
        mesh=mesh,
        in_specs=(
            P("gx", "gy", None, None),
            P("gx", "gy", None, None, None),
            P(None, "gx", "gy", None, None),
            P("gx", "gy", None),
            P(None, "gy", None, None),
            P(None, "gy", None, None),
            P(),
            P("gx", "gy", None, None),
        ),
        out_specs=(P("gx", "gy", None, None), P("gx", "gy", None, None)),
        check_vma=False,
    )
```

```python
import functools

import jax
import jax.numpy as jnp
from jax import lax
from jax.experimental import pallas as pl
from jax.experimental.pallas import tpu as pltpu
from jax.sharding import PartitionSpec as P

MESH = pl.DeviceIdType.MESH
PART, ALONG_X, ALONG_Y, X_PART, Y_PART, DIAG, D_PART = range(7)


def padded(x, sides, width):
    for axis, dim in sides:
        size, length = (lax.axis_size(axis), x.shape[dim])
        up = [(i, (i + 1) % size) for i in range(size - 1)]
        down = [(j, i) for i, j in up]
        last = lax.slice_in_dim(x, length - width, length, axis=dim)
        first = lax.slice_in_dim(x, 0, width, axis=dim)
        before = lax.ppermute(last, axis, up)
        after = lax.ppermute(first, axis, down)
        x = jnp.concatenate([before, x, after], axis=dim)
    return x


def shards(state, weights, drive, leak, link_dev, link_blk, offsets, gram_prev):
    grid_rows, grid_cols, batch_cols, units = state.shape
    nblocks = grid_rows * grid_cols
    nlinks = link_dev.shape[-1]
    nstencil = offsets.shape[0]
    gx_size = lax.axis_size("gx")
    own_index = lax.axis_index("gx")
    all_dev = link_dev[:, 0].reshape(gx_size, nblocks * nlinks)
    all_blk = link_blk[:, 0].reshape(gx_size, nblocks * nlinks)
    my_dev = lax.dynamic_index_in_dim(all_dev, own_index, 0, keepdims=False)
    my_blk = lax.dynamic_index_in_dim(all_blk, own_index, 0, keepdims=False)
    w_long = weights[:, :, nstencil : nstencil + nlinks].reshape(nblocks, nlinks, units, units)
    current = state
    gram = gram_prev
    for step_id in range(drive.shape[0]):
        extended = padded(current, (("gx", 0), ("gy", 1)), 1)
        preact = jnp.zeros((grid_rows, grid_cols, batch_cols, units), jnp.float32)
        for offset_id in range(nstencil):
            zero = jnp.zeros((), jnp.int32)
            start_r = 1 + offsets[offset_id, 0]
            start_c = 1 + offsets[offset_id, 1]
            nearby = lax.dynamic_slice(
                extended, (start_r, start_c, zero, zero), (grid_rows, grid_cols, batch_cols, units)
            )
            preact = preact + jnp.einsum(
                "rcsu,rcuv->rcsv",
                nearby,
                weights[:, :, offset_id],
                preferred_element_type=jnp.float32,
            )
        flat_state = current.reshape(nblocks, batch_cols, units)
        whole = lax.all_gather(flat_state[None], "gx", axis=0, tiled=True)
        picked = whole.reshape(gx_size * nblocks, batch_cols, units)[my_dev * nblocks + my_blk]
        picked = picked.reshape(nblocks, nlinks, batch_cols, units)
        distant = jnp.einsum("blsu,bluv->bsv", picked, w_long, preferred_element_type=jnp.float32)
        preact = preact + distant.reshape(grid_rows, grid_cols, batch_cols, units)
        preact = preact + jnp.einsum(
            "rcsu,rcuv->rcsv",
            drive[step_id],
            weights[:, :, nstencil + nlinks],
            preferred_element_type=jnp.float32,
        )
        rate = leak[:, :, None, :]
        current = ((1.0 - rate) * current.astype(jnp.float32) + rate * jnp.tanh(preact)).astype(
            jnp.bfloat16
        )
        gram = gram + jnp.einsum(
            "rcsu,rcsv->rcuv", current, current, preferred_element_type=jnp.float32
        )
    return (current, gram)


def reservoir(
    n_gy, state, w, drive, leak, ldev, lblk, offs, gprev, out, gout,
    gath00, gath01, gath10, gath11, ext00, ext01, ext10, ext11, wv, dv, gv, acc, xf,
    load_sem, store_sem, send_sem, recv_sem, zsend_sem, zrecv_sem,
):
    rows, cols, seq, units = state.shape
    nstencil, nlinks = offs.shape[1], ldev.shape[1]
    half = seq // 2
    g, b = lax.axis_index("gx"), lax.axis_index("gy")
    core, x, y = lax.rem(g, 2), lax.rem(lax.div(g, 2), 2), lax.div(g, 4)
    near = lambda fy, fx, fc: (
        (1 - y if fy else y) * 4 + (1 - x if fx else x) * 2 + (1 - core if fc else core)
    )
    ids = {
        PART: near(0, 0, 1), ALONG_X: near(0, 1, 0), ALONG_Y: near(1, 0, 0),
        X_PART: near(0, 1, 1), Y_PART: near(1, 0, 1), DIAG: near(1, 1, 0), D_PART: near(1, 1, 1),
    }
    has_left, has_right = b > 0, b < n_gy - 1
    has_up, has_down = g > 0, g < 7
    gaths, exts = (gath00, gath01, gath10, gath11), (ext00, ext01, ext10, ext11)

    loads = []

    def load(src, dst):
        copy = pltpu.make_async_copy(src, dst, load_sem.at[len(loads)])
        copy.start()
        loads.append(copy)
        return copy

    for r in range(rows):
        for s in (0, 1):
            load(state.at[r, :, pl.ds(s * half, half)], gaths[s].at[g, pl.ds(r * cols, cols)])

    barrier = pltpu.get_barrier_semaphore()
    for rel in (PART, ALONG_X, ALONG_Y):
        pl.semaphore_signal(barrier, inc=1, device_id={"gx": ids[rel]}, device_id_type=MESH)

    @pl.when(has_left)
    def _():
        pl.semaphore_signal(barrier, inc=1, device_id={"gy": b - 1}, device_id_type=MESH)

    @pl.when(has_right)
    def _():
        pl.semaphore_signal(barrier, inc=1, device_id={"gy": b + 1}, device_id_type=MESH)

    inside = jnp.logical_and(has_left, has_right)

    @pl.when(inside)
    def _():
        pl.semaphore_wait(barrier, 5)

    @pl.when(jnp.logical_not(inside))
    def _():
        pl.semaphore_wait(barrier, 4 if n_gy > 1 else 3)

    sends = []

    def send(t, rel_from, r, to, rel_there):
        origin = g if rel_from is None else ids[rel_from]
        here = gaths[t].at[origin, pl.ds(r * cols, cols)]
        src = state.at[r, :, pl.ds(t * half, half)] if rel_from is None and t < 2 else here
        copy = pltpu.make_async_remote_copy(
            src_ref=src, dst_ref=here,
            send_sem=send_sem.at[len(sends)], recv_sem=recv_sem.at[t, rel_there, r],
            device_id={"gx": ids[to]}, device_id_type=MESH,
        )
        copy.start()
        sends.append(copy)

    def send_own(t, r, to):
        send(t, None, r, to, to)

    def arrived(t, rel, r):
        here = gaths[t].at[ids[rel], pl.ds(r * cols, cols)]
        pltpu.make_async_remote_copy(
            src_ref=here, dst_ref=here,
            send_sem=send_sem.at[0], recv_sem=recv_sem.at[t, rel, r],
            device_id={"gx": ids[PART]}, device_id_type=MESH,
        ).wait_recv()

    def relay(t, rel, r, across=None):
        arrived(t, rel, r)
        if across is not None:
            send(t, rel, r, across, DIAG)
        send(t, rel, r, PART, {ALONG_X: X_PART, ALONG_Y: Y_PART, DIAG: D_PART}[rel])

    def rim_copy(t, side, kind):
        col = 0 if side == 0 else cols - 1
        there = cols + 1 if side == 0 else 0
        gath, ext = gaths[t], exts[t]
        if kind == 0:
            return [
                pltpu.make_async_remote_copy(
                    src_ref=state.at[r, col, pl.ds(t * half, half)]
                    if t < 2
                    else gath.at[g, r * cols + col],
                    dst_ref=ext.at[r + 1, there],
                    send_sem=zsend_sem.at[t, side, r], recv_sem=zrecv_sem.at[t, side, r],
                    device_id={"gy": b - 1 if side == 0 else b + 1}, device_id_type=MESH,
                )
                for r in range(rows)
            ]
        src = (
            gath.at[lax.rem(g + 7, 8), (rows - 1) * cols + col]
            if kind == 1
            else gath.at[lax.rem(g + 1, 8), col]
        )
        return [
            pltpu.make_async_remote_copy(
                src_ref=src,
                dst_ref=ext.at[0 if kind == 1 else rows + 1, there],
                send_sem=zsend_sem.at[t, side, rows + kind - 1],
                recv_sem=zrecv_sem.at[t, side, rows + kind - 1],
                device_id={"gy": b - 1 if side == 0 else b + 1}, device_id_type=MESH,
            )
        ]

    def rims(t, do, kinds):
        for side in (0, 1):
            present = (has_left, has_right)
            who = present[side] if do != "wait_recv" else present[1 - side]
            for kind in kinds:
                cond = who
                if kind == 1:
                    cond = jnp.logical_and(who, has_up)
                if kind == 2:
                    cond = jnp.logical_and(who, has_down)

                @pl.when(cond)
                def _():
                    for copy in rim_copy(t, side, kind):
                        getattr(copy, do)()

    def begin(t, r):
        if r != 2:
            send_own(t, r, ALONG_X)
        if r != 1:
            send_own(t, r, ALONG_Y)
        send_own(t, r, PART)

    def exchange(t):
        relay(t, ALONG_X, 0, ALONG_Y)
        send_own(t, 1, ALONG_Y)
        relay(t, ALONG_Y, 0)
        relay(t, ALONG_X, 3)
        relay(t, ALONG_Y, 3, ALONG_X)
        send_own(t, 2, ALONG_X)
        relay(t, ALONG_X, 1, ALONG_Y)
        relay(t, ALONG_Y, 2, ALONG_X)

    def borders(t):
        relay(t, DIAG, 0)
        relay(t, DIAG, 3)
        for rel in (PART, X_PART, D_PART):
            arrived(t, rel, 0)
            arrived(t, rel, 3)
        rims(t, "start", (1, 2))
        fill(t)
        rims(t, "wait_recv", (0, 1, 2))

    def finish(t):
        relay(t, ALONG_Y, 1)
        relay(t, ALONG_X, 2)
        relay(t, DIAG, 1)
        relay(t, DIAG, 2)
        for rel in (PART, X_PART, D_PART):
            arrived(t, rel, 1)
            arrived(t, rel, 2)
        for r in range(rows):
            arrived(t, Y_PART, r)

    def fill(t):
        gath, ext = gaths[t], exts[t]

        def place(i, carry):
            r, c = i // cols, lax.rem(i, cols)
            ext[r + 1, c + 1] = gath[g, i]
            return carry

        lax.fori_loop(0, rows * cols, place, 0)
        zero = jnp.zeros((half, units), jnp.bfloat16)

        @pl.when(has_up)
        def _():
            for c in range(cols):
                ext[0, c + 1] = gath[lax.rem(g + 7, 8), (rows - 1) * cols + c]

        @pl.when(has_down)
        def _():
            for c in range(cols):
                ext[rows + 1, c + 1] = gath[lax.rem(g + 1, 8), c]

        for there, edge in ((0, has_up), (rows + 1, has_down)):

            @pl.when(jnp.logical_not(edge))
            def _():
                for c in range(cols + 2):
                    ext[there, c] = zero

        for there, side in ((0, has_left), (cols + 1, has_right)):

            @pl.when(jnp.logical_not(side))
            def _():
                for r in range(rows):
                    ext[r + 1, there] = zero
                for r, edge in ((0, has_up), (rows + 1, has_down)):

                    @pl.when(edge)
                    def _():
                        ext[r, there] = zero

    def dot(a, weight):
        return jnp.dot(a, weight, preferred_element_type=jnp.float32)

    def nearby(t):
        ext = exts[t]

        def one(i, carry):
            r, c = i // cols, lax.rem(i, cols)
            total = dot(
                dv[t // 2, r, c, pl.ds(t % 2 * half, half)], wv[r, c, nstencil + nlinks]
            )
            for k in range(nstencil):
                total = total + dot(ext[r + 1 + offs[0, k], c + 1 + offs[1, k]], wv[r, c, k])
            acc[i] = total
            return carry

        lax.fori_loop(0, rows * cols, one, 0)

    def gram_of(r, c, now):
        gv[r, c] += lax.dot_general(
            now, now, (((0,), (0,)), ((), ())), preferred_element_type=jnp.float32
        )

    def distant(t, r):
        gath = gaths[t]

        def one(c, carry):
            i = r * cols + c
            total = acc[i]
            for l in range(nlinks):
                total = total + dot(gath[ldev[g, l, 0, i], lblk[g, l, 0, i]], wv[r, c, nstencil + l])
            rate = leak[c, pl.ds(r, 1), :]
            old = gath[g, i].astype(jnp.float32)
            now = ((1.0 - rate) * old + rate * jnp.tanh(total)).astype(jnp.bfloat16)
            if t >= 2:
                xf[i, pl.ds((t - 2) * half, half)] = now
            else:
                gaths[t + 2][g, i] = now
            if t < 3:
                gram_of(r, c, now)
            return carry

        lax.fori_loop(0, cols, one, 0)

    order = (0, 3, 1, 2)

    def start(t):
        for r in order:
            begin(t, r)
        rims(t, "start", (0,))

    stores = []

    def store(src, dst):
        copy = pltpu.make_async_copy(src, dst, store_sem.at[len(stores)])
        copy.start()
        stores.append(copy)

    start(0)
    for r in range(rows):
        load(w.at[r], wv.at[r])
    load(drive, dv)
    load(gprev, gv)
    for t in range(4):
        exchange(t)
        if t < 3:
            start(t + 1)
        if t == 0:
            for copy in loads:
                copy.wait()
        borders(t)
        nearby(t)
        finish(t)
        for r in range(rows):
            distant(t, r)
            if t == 3:
                store(xf.at[pl.ds(r * cols, cols)], out.at[r])
        if t == 2:
            store(gv, gout)
    for copy in sends:
        copy.wait_send()
    for t in range(4):
        rims(t, "wait_send", (0, 1, 2))
    for copy in stores:
        copy.wait()


def closing(half, x, gram, out, gout, xv, gv, x_sem, g_sem, out_sem, gout_sem):
    rows, cols = x.shape[:2]
    copy = pltpu.make_async_copy
    x_in = [copy(x.at[r], xv.at[r], x_sem.at[r]) for r in range(rows)]
    g_in = [copy(gram.at[r], gv.at[r], g_sem.at[r]) for r in range(rows)]
    x_out = [copy(xv.at[r], out.at[r], out_sem.at[r]) for r in range(rows)]
    g_out = [copy(gv.at[r], gout.at[r], gout_sem.at[r]) for r in range(rows)]
    for r in range(rows):
        x_in[r].start()
        g_in[r].start()
    for r in range(rows):
        x_in[r].wait()
        x_out[r].start()
        g_in[r].wait()
        for c in range(cols):
            now = xv[r, c, pl.ds(half, half)]
            gv[r, c] += lax.dot_general(
                now, now, (((0,), (0,)), ((), ())), preferred_element_type=jnp.float32
            )
        g_out[r].start()
    for r in range(rows):
        x_out[r].wait()
        g_out[r].wait()


LEVELS = ((13, 8), (12, 7))
SLOTS, AHEAD = 13, 5
LANES = 16


def route(ldev, lblk, spot, pick):
    rows_of = lambda n: lax.broadcasted_iota(jnp.int32, (n, 128), 0)
    lanes_of = lambda n: lax.broadcasted_iota(jnp.int32, (n, 128), 1)
    nlinks, nblocks = ldev.shape[1], ldev.shape[3]
    g = lax.axis_index("gx")
    core, home = g % 2, g // 2
    lane = lanes_of(8)
    chip, block = lane // 32, lane % LANES

    needs = []
    for c in range(4):
        need = jnp.zeros((8, 128), jnp.bool_)
        for a in (2 * c, 2 * c + 1):
            for l in range(nlinks):
                for q in range(nblocks):
                    need = need | (lane == ldev[a, l, 0, q] * LANES + lblk[a, l, 0, q])
        for src, dst in ((2 * c - 1, 2 * c), (2 * c + 2, 2 * c + 1)):
            if 0 <= src < 8:
                first = nblocks - 3 if src < dst else 0
                need = need | ((lane >= src * LANES + first) & (lane < src * LANES + first + 3))
        needs.append(need.astype(jnp.int32))

    def seen(flip):
        return jnp.where(
            chip == 0, needs[flip],
            jnp.where(chip == 1, needs[1 ^ flip], jnp.where(chip == 2, needs[2 ^ flip], needs[3 ^ flip])),
        )

    nx, ny, nd = seen(1), seen(2), seen(3)
    only_x, both, neither, only_y = nd * nx * (1 - ny), nd * nx * ny, nd * (1 - nx) * (1 - ny), nd * ny * (1 - nx)
    classes = [only_x, both, neither, only_y, nx, ny]

    def stack(parts):
        sub, stacked = rows_of(8), jnp.zeros((8, 128), jnp.int32)
        for k, part in enumerate(parts):
            stacked = jnp.where(sub == k, part, stacked)
        return stacked.astype(jnp.float32)

    def times(x, matrix):
        return jnp.dot(
            x.astype(jnp.bfloat16), matrix.astype(jnp.float32).astype(jnp.bfloat16),
            preferred_element_type=jnp.float32,
        ).astype(jnp.int32)

    above, across = rows_of(128), lanes_of(128)
    upto = (above <= across) & (above // 32 == across // 32)
    counted = stack(classes)
    sums = times(counted, upto)
    totals = [times(counted, above // 32 == c) for c in range(4)]
    row = lambda x, k: jnp.broadcast_to(x[k : k + 1], (8, 128))

    cand = rows_of(32) * 128 + lanes_of(32)
    wide = lambda c, k: jnp.broadcast_to(totals[c][k : k + 1], (32, 128))
    fx, fy, rx, ry = [], [], [], []

    def passed(counts, digit):
        total = counts[0] + counts[1] + counts[2] + counts[3]
        start = (2 * counts[0] + counts[1] + counts[2] + 1) // 2 - 4
        return total, jnp.maximum(jnp.minimum(start + digit, total), 0)

    for c in range(4):
        counts = [wide(c, k) for k in range(6)]
        total, m = passed(counts, (cand >> (3 * c)) & 7)
        rest = total - m
        rx.append(m)
        ry.append(rest)
        fx.append(counts[4] + jnp.maximum(m - counts[0] - counts[1], 0))
        fy.append(
            counts[5] + jnp.maximum(jnp.minimum(rest - counts[3], counts[2]), 0)
            + jnp.maximum(rest - counts[3] - counts[2] - counts[1], 0)
        )
    worst = jnp.zeros((32, 128), jnp.int32)
    for c in range(4):
        worst = jnp.maximum(worst, fx[c] + ry[c ^ 2])
        worst = jnp.maximum(worst, fy[c] + rx[c ^ 1])
        worst = jnp.where(jnp.maximum(rx[c], ry[c]) > 2 * AHEAD, 255, worst)
    best = jnp.min(worst * 4096 + cand)

    pickc = lambda values: jnp.where(
        chip == 0, values[0], jnp.where(chip == 1, values[1], jnp.where(chip == 2, values[2], values[3]))
    )
    count = [pickc([row(totals[c], k) for c in range(4)]) for k in range(6)]
    digit = pickc([(best >> (3 * c)) & 7 for c in range(4)])
    total, m = passed(count, digit)
    rank = jnp.where(
        only_x > 0, row(sums, 0) - 1,
        jnp.where(
            both > 0, count[0] + row(sums, 1) - 1,
            jnp.where(
                neither > 0, count[0] + count[1] + row(sums, 2) - 1,
                count[0] + count[1] + count[2] + row(sums, 3) - 1,
            ),
        ),
    )
    via_x = jnp.where(rank < m, nd, 0)
    via_y = nd - via_x
    more = times(stack([nx * (1 - via_x), ny * (1 - via_y)]), upto)
    over = rank - m
    pos_x = jnp.where(via_x > 0, rank, m + row(more, 0) - 1)
    pos_y = jnp.where(via_y > 0, over, total - m + row(more, 1) - 1)
    held_x, held_y = jnp.maximum(nx, via_x), jnp.maximum(ny, via_y)

    mine = block + jnp.where((lane // LANES) % 2 == core, 0, 12)
    base = 2 * nblocks
    inward = lambda link, k, p: base + 2 * SLOTS * link + jnp.where(k == core, 0, SLOTS) + p
    odd = lambda x: x & 1
    where_to = lambda slots: jnp.where(
        chip == home, mine,
        jnp.where(
            chip == (home ^ 1), inward(0, odd(pos_x), pos_x >> 1),
            jnp.where(
                chip == (home ^ 2), inward(1, odd(pos_y + 1), pos_y >> 1),
                jnp.where(
                    via_x > 0, inward(1, odd(rank), slots - 1 - (rank >> 1)),
                    inward(0, odd(over + 1), slots - 1 - (over >> 1)),
                ),
            ),
        ),
    )
    there = where_to(LEVELS[0][0])
    for n, (slots, _) in enumerate(LEVELS):
        there = jnp.where(rows_of(8) == n, where_to(slots), there)
    spot[...] = jnp.maximum(jnp.minimum(there, base + 4 * SLOTS - 1), 0)

    sub = rows_of(32)
    place, is_y = sub % 16, sub >= 16
    full = lambda x: jnp.broadcast_to(x[0:1], (32, 128))
    own_chip = full(jnp.where(chip == home, 1, 0)) > 0
    own_at = jnp.where(is_y, full(pos_y), full(pos_x))
    own_core = jnp.where(is_y, odd(own_at + 1), odd(own_at))
    own_held = jnp.where(is_y, full(held_y), full(held_x)) > 0
    own_hit = own_chip & own_held & (own_at >> 1 == place) & (own_core == core)
    pass_x = full(jnp.where(chip == (home ^ 2), via_y, 0))
    pass_y = full(jnp.where(chip == (home ^ 1), via_x, 0))
    pass_held = jnp.where(is_y, pass_y, pass_x) > 0
    pass_rank = jnp.where(is_y, full(rank), full(over))
    pass_core = jnp.where(is_y, odd(pass_rank), odd(pass_rank + 1))
    for n, (slots, first) in enumerate(LEVELS):
        pass_hit = pass_held & (slots - 1 - (pass_rank >> 1) == place) & (pass_core == core)
        value = jnp.where(own_hit, full(mine), 0) + jnp.where(pass_hit, base + (pass_rank >> 1), 0)
        value = jnp.sum(value.astype(jnp.float32), axis=1, keepdims=True).astype(jnp.int32)
        value = jnp.broadcast_to(value, (32, 128))
        most = jnp.where(place < first, base - 1, base + AHEAD - 1)
        pick[n] = jnp.maximum(jnp.minimum(value, most), 0)
    least = jnp.zeros((8, 128), jnp.int32) + (best >> 12)
    level = jnp.zeros((8, 128), jnp.int32)
    for n, (slots, _) in enumerate(LEVELS):
        level = jnp.where(least <= 2 * slots, n + 1, level)
    return level


def agree(n_gy, ldev, lblk, state, spot, pick, verdict, peer, votes, send_sem, recv_sem):
    g, b = lax.axis_index("gx"), lax.axis_index("gy")
    part = g + 1 - 2 * lax.rem(g, 2)
    barrier = pltpu.get_barrier_semaphore()
    pl.semaphore_signal(barrier, inc=1, device_id={"gx": part}, device_id_type=MESH)
    for d in range(1, n_gy):
        pl.semaphore_signal(barrier, inc=1, device_id={"gy": lax.rem(b + d, n_gy)}, device_id_type=MESH)
    votes[0] = route(ldev, lblk, spot, pick)
    pl.semaphore_wait(barrier, n_gy)
    copies = []
    for d in range(1, n_gy):
        copies.append(pltpu.make_async_remote_copy(
            src_ref=votes.at[0], dst_ref=votes.at[d], send_sem=send_sem.at[d], recv_sem=recv_sem.at[d],
            device_id={"gy": lax.rem(b + d, n_gy)}, device_id_type=MESH,
        ))
    copies.append(pltpu.make_async_remote_copy(
        src_ref=state, dst_ref=peer, send_sem=send_sem.at[0], recv_sem=recv_sem.at[0],
        device_id={"gx": part}, device_id_type=MESH,
    ))
    for copy in copies:
        copy.start()
    for copy in copies:
        copy.wait()
    verdict[0, 0] = jnp.min(jnp.min(votes[...], axis=0))


def routed(
    n_gy, level, state, peer, w, drive, leak, spot, pick, ldev, lblk, offs, gprev, out, gout,
    own0, own1, own2, own3, gath0, gath1, gath2, gath3,
    headx0, headx1, headx2, headx3, heady0, heady1, heady2, heady3,
    early, late, side, corner, mid, top, bot, wv, dv, gv, acc, xf,
    load_sem, store_sem, local_sem, link_send, link_recv, pass_send, pass_recv, peer_send, peer_recv,
    zsend_sem, zrecv_sem,
):
    slots, first = LEVELS[level]
    seq, units = state.shape[1:]
    rows, cols = w.shape[:2]
    blocks = rows * cols
    nstencil, nlinks = offs.shape[1], ldev.shape[1]
    half = seq // 2
    base = 2 * blocks
    g, b = lax.axis_index("gx"), lax.axis_index("gy")
    core, x, y = lax.rem(g, 2), lax.rem(lax.div(g, 2), 2), lax.div(g, 4)
    part = y * 4 + x * 2 + 1 - core
    along = (y * 4 + (1 - x) * 2 + core, (1 - y) * 4 + x * 2 + core)
    has_left, has_right = b > 0, b < n_gy - 1
    has_up, has_down = g > 0, g < 7
    owns, gaths = (own0, own1, own2, own3), (gath0, gath1, gath2, gath3)
    heads = ((headx0, headx1, headx2, headx3), (heady0, heady1, heady2, heady3))

    def local(src, dst, sem):
        copy = pltpu.make_async_copy(src, dst, sem)
        copy.start()
        return copy

    firsts = []
    for t in (0, 1):
        firsts.append([
            local(state.at[:, pl.ds(t * half, half)], owns[t].at[pl.ds(0, blocks)], load_sem.at[2 * t]),
            local(peer.at[:, pl.ds(t * half, half)], owns[t].at[pl.ds(blocks, blocks)], load_sem.at[2 * t + 1]),
        ])

    barrier = pltpu.get_barrier_semaphore()
    for to in (part, *along):
        pl.semaphore_signal(barrier, inc=1, device_id={"gx": to}, device_id_type=MESH)

    @pl.when(has_left)
    def _():
        pl.semaphore_signal(barrier, inc=1, device_id={"gy": b - 1}, device_id_type=MESH)

    @pl.when(has_right)
    def _():
        pl.semaphore_signal(barrier, inc=1, device_id={"gy": b + 1}, device_id_type=MESH)

    inside = jnp.logical_and(has_left, has_right)

    @pl.when(inside)
    def _():
        pl.semaphore_wait(barrier, 5)

    @pl.when(jnp.logical_not(inside))
    def _():
        pl.semaphore_wait(barrier, 4 if n_gy > 1 else 3)

    bounds = ((0, AHEAD), (AHEAD, first), (first, slots))

    def region(t, link, lead, part_id):
        low, high = bounds[part_id]
        return gaths[t].at[pl.ds(base + 2 * SLOTS * link + (0 if lead else SLOTS) + low, high - low)]

    def link_copy(t, link, part_id):
        low, high = bounds[part_id]
        src = late.at[t, link] if part_id == 2 else early.at[t, link, pl.ds(low, high - low)]
        dst = heads[link][t] if part_id == 0 else region(t, link, True, part_id)
        return pltpu.make_async_remote_copy(
            src_ref=src, dst_ref=dst, send_sem=link_send.at[t, link, part_id], recv_sem=link_recv.at[t, link, part_id],
            device_id={"gx": along[link]}, device_id_type=MESH,
        )

    def pass_copy(t, link, part_id):
        src = heads[link][t] if part_id == 0 else region(t, link, True, part_id)
        return pltpu.make_async_remote_copy(
            src_ref=src, dst_ref=region(t, link, False, part_id),
            send_sem=pass_send.at[t, link, part_id], recv_sem=pass_recv.at[t, link, part_id],
            device_id={"gx": part}, device_id_type=MESH,
        )

    def head_copy(t, link):
        return pltpu.make_async_copy(heads[link][t], region(t, link, True, 0), local_sem.at[t, link])

    def own_copy(t):
        return pltpu.make_async_copy(owns[t], gaths[t].at[pl.ds(0, base)], local_sem.at[t, 2])

    def peer_copy(t, r):
        return pltpu.make_async_remote_copy(
            src_ref=owns[t].at[pl.ds(r * cols, cols)], dst_ref=owns[t].at[pl.ds(blocks + r * cols, cols)],
            send_sem=peer_send.at[t - 2, r], recv_sem=peer_recv.at[t - 2, r],
            device_id={"gx": part}, device_id_type=MESH,
        )

    def rim_copy(t, to, r):
        src = owns[t].at[r * cols + (0 if to == 0 else cols - 1)] if r < rows else corner.at[t, to, r - rows]
        return pltpu.make_async_remote_copy(
            src_ref=src, dst_ref=side.at[t, 1 - to, r],
            send_sem=zsend_sem.at[t, to, r], recv_sem=zrecv_sem.at[t, 1 - to, r],
            device_id={"gy": b - 1 if to == 0 else b + 1}, device_id_type=MESH,
        )

    def rim_wait(t, came, r):
        pltpu.make_async_remote_copy(
            src_ref=side.at[t, came, r], dst_ref=side.at[t, came, r],
            send_sem=zsend_sem.at[t, came, r], recv_sem=zrecv_sem.at[t, came, r],
            device_id={"gy": b - 1 if came == 0 else b + 1}, device_id_type=MESH,
        ).wait_recv()

    def rims(t, do, corners):
        for s, present in ((0, has_left), (1, has_right)):
            for r in ((rows, rows + 1) if corners else range(rows)):
                cond = present
                if corners:
                    cond = jnp.logical_and(present, has_up if r == rows else has_down)

                @pl.when(cond)
                def _():
                    do(t, s, r)

    def begin(t):
        for j in range(first):
            for link in (0, 1):
                early[t, link, j] = owns[t][pick[level, 16 * link + j, 0]]
            if j == AHEAD - 1:
                for link in (0, 1):
                    link_copy(t, link, 0).start()
        for link in (0, 1):
            link_copy(t, link, 1).start()
        rims(t, lambda *at: rim_copy(*at).start(), False)
        own_copy(t).start()

    def follow(t):
        for link in (0, 1):
            link_copy(t, link, 0).wait_recv()
        for link in (0, 1):
            for j in range(slots - first):
                at = pick[level, 16 * link + first + j, 0]
                passing = at >= base
                one = owns[t][jnp.where(passing, 0, at)]
                two = heads[1 - link][t][jnp.where(passing, at - base, 0)]
                late[t, link, j] = jnp.where(passing, two, one)
            link_copy(t, link, 2).start()
        for link in (0, 1):
            pass_copy(t, link, 0).start()
            head_copy(t, link).start()

    def relay(t, part_id):
        for link in (0, 1):
            link_copy(t, link, part_id).wait_recv()
            pass_copy(t, link, part_id).start()

    def settle(t):
        own_copy(t).wait()
        for link in (0, 1):
            head_copy(t, link).wait()
            for part_id in range(3):
                pass_copy(t, link, part_id).wait_recv()

    def dot(a, weight):
        return jnp.dot(a, weight, preferred_element_type=jnp.float32)

    def clear():
        zero = jnp.zeros((half, units), jnp.bfloat16)

        @pl.when(jnp.logical_not(has_up))
        def _():
            for c in range(cols + 2):
                top[0, c] = zero

        @pl.when(jnp.logical_not(has_down))
        def _():
            for c in range(cols + 2):
                bot[2, c] = zero

        for at, present in ((0, has_left), (cols + 1, has_right)):

            @pl.when(jnp.logical_not(present))
            def _():
                for r in range(rows):
                    mid[r, at] = zero
                for r in range(3):
                    top[r, at] = zero
                    bot[r, at] = zero

    def put(r, at, value):
        mid[r, at] = value
        if r < 2:
            top[r + 1, at] = value
        if r >= rows - 2:
            bot[r - rows + 2, at] = value

    def fill_mid(t):
        for r in range(rows):
            for c in range(cols):
                put(r, c + 1, owns[t][r * cols + c])
        for s, present in ((0, has_left), (1, has_right)):

            @pl.when(present)
            def _():
                for r in range(rows):
                    put(r, 0 if s == 0 else cols + 1, side[t, s, r])

    def fill_rims(t):
        gath = gaths[t]
        for up, present in ((True, has_up), (False, has_down)):

            @pl.when(present)
            def _():
                for c in range(cols):
                    src = (g - 1) * LANES + (rows - 1) * cols + c if up else (g + 1) * LANES + c
                    value = gath[spot[level, src]]
                    if up:
                        top[0, c + 1] = value
                    else:
                        bot[2, c + 1] = value
                    for to, col in ((0, 0), (1, cols - 1)):
                        if c == col:
                            corner[t, to, 0 if up else 1] = value

    def fill_corners(t):
        for s, has in ((0, has_left), (1, has_right)):
            at = 0 if s == 0 else cols + 1

            @pl.when(jnp.logical_and(has, has_up))
            def _():
                top[0, at] = side[t, s, rows]

            @pl.when(jnp.logical_and(has, has_down))
            def _():
                bot[2, at] = side[t, s, rows + 1]

    def over(r, body):
        def one(c, carry):
            body(c, r * cols + c)
            return carry

        lax.fori_loop(0, cols, one, 0)

    def driven(t, r, c):
        return dot(dv[t // 2, r, c, pl.ds(t % 2 * half, half)], wv[r, c, nstencil + nlinks])

    def nearby(total, r, c, near, shift):
        for k in range(nstencil):
            total = total + dot(near[r + shift + offs[0, k], c + 1 + offs[1, k]], wv[r, c, k])
        return total

    def distant(total, t, r, c):
        i = r * cols + c
        for l in range(nlinks):
            src = spot[level, ldev[g, l, 0, i] * LANES + lblk[g, l, 0, i]]
            total = total + dot(gaths[t][src], wv[r, c, nstencil + l])
        return total

    def renew(total, t, r, c):
        i = r * cols + c
        rate = leak[c, pl.ds(r, 1), :]
        old = owns[t][i].astype(jnp.float32)
        now = ((1.0 - rate) * old + rate * jnp.tanh(total)).astype(jnp.bfloat16)
        if t >= 2:
            xf[i, pl.ds((t - 2) * half, half)] = now
        else:
            owns[t + 2][i] = now

    def keep(i, total):
        acc[i] = total

    def gram_of(t):
        def one(i, carry):
            now = owns[t + 2][i] if t < 2 else xf[i, pl.ds(0, half)]
            r, c = i // cols, lax.rem(i, cols)
            gv[r, c] += lax.dot_general(now, now, (((0,), (0,)), ((), ())), preferred_element_type=jnp.float32)
            return carry

        lax.fori_loop(0, blocks, one, 0)

    loads, stores = [], []

    def finished(t, r):
        if t < 2:
            peer_copy(t + 2, r).start()
        if t == 3:
            stores.append(local(xf.at[pl.ds(r * cols, cols)], out.at[r], store_sem.at[1 + r]))

    for copy in firsts[0]:
        copy.wait()
    begin(0)
    for copy in firsts[1]:
        copy.wait()
    for r in range(rows):
        loads.append(local(w.at[r], wv.at[r], load_sem.at[4 + r]))
    loads.append(local(drive, dv, load_sem.at[4 + rows]))
    loads.append(local(gprev, gv, load_sem.at[5 + rows]))
    clear()
    follow(0)
    begin(1)
    for copy in loads:
        copy.wait()
    inner, outer = range(1, rows - 1), ((0, top, 1), (rows - 1, bot, 2 - rows))
    for t in range(4):
        rims(t, rim_wait, False)
        fill_mid(t)
        relay(t, 1)
        for r in inner:
            over(r, lambda c, i: keep(i, nearby(driven(t, r, c), r, c, mid, 0)))
        relay(t, 2)
        for r, _, _ in outer:
            over(r, lambda c, i: keep(i, driven(t, r, c)))
        if t in (1, 2):
            gram_of(t - 1)
        settle(t)
        fill_rims(t)
        rims(t, lambda *at: rim_copy(*at).start(), True)
        for r in inner:
            over(r, lambda c, i: renew(distant(acc[i], t, r, c), t, r, c))
            finished(t, r)
        for r, _, _ in outer:
            over(r, lambda c, i: keep(i, distant(acc[i], t, r, c)))
        if t < 3:
            follow(t + 1)
        rims(t, rim_wait, True)
        fill_corners(t)
        for r, near, shift in outer:
            over(r, lambda c, i: renew(nearby(acc[i], r, c, near, shift), t, r, c))
            finished(t, r)
        if t < 2:
            for r in range(rows):
                peer_copy(t + 2, r).wait_recv()
            begin(t + 2)
        if t == 2:
            gram_of(t)
        if t == 2:
            stores.append(local(gv, gout, store_sem.at[0]))
    for t in range(4):
        for link in (0, 1):
            for part_id in range(3):
                link_copy(t, link, part_id).wait_send()
                pass_copy(t, link, part_id).wait_send()
        rims(t, lambda *at: rim_copy(*at).wait_send(), False)
        rims(t, lambda *at: rim_copy(*at).wait_send(), True)
        if t >= 2:
            for r in range(rows):
                peer_copy(t, r).wait_send()
    for copy in stores:
        copy.wait()


def general(n_gy, state, weights, drive, leak, link_dev, link_blk, offsets, gram_prev):
    rows, cols, seq, units = state.shape
    blocks = rows * cols
    anywhere = pl.BlockSpec(memory_space=pl.ANY)
    scalars = pl.BlockSpec(memory_space=pltpu.SMEM)
    block = (seq // 2, units)
    return pl.pallas_call(
        functools.partial(reservoir, n_gy),
        out_shape=(
            jax.ShapeDtypeStruct(state.shape, state.dtype),
            jax.ShapeDtypeStruct(gram_prev.shape, gram_prev.dtype),
        ),
        in_specs=[
            anywhere, anywhere, anywhere, pl.BlockSpec(memory_space=pltpu.VMEM),
            scalars, scalars, scalars, anywhere,
        ],
        out_specs=(anywhere, anywhere),
        scratch_shapes=[
            *[pltpu.VMEM((8, blocks, *block), jnp.bfloat16)] * 4,
            *[pltpu.VMEM((rows + 2, cols + 2, *block), jnp.bfloat16)] * 4,
            pltpu.VMEM(weights.shape, weights.dtype),
            pltpu.VMEM(drive.shape, drive.dtype),
            pltpu.VMEM(gram_prev.shape, gram_prev.dtype),
            pltpu.VMEM((blocks, *block), jnp.float32),
            pltpu.VMEM((blocks, seq, units), jnp.bfloat16),
            pltpu.SemaphoreType.DMA((14,)),
            pltpu.SemaphoreType.DMA((8,)),
            pltpu.SemaphoreType.DMA((112,)),
            pltpu.SemaphoreType.DMA((4, 7, 4)),
            pltpu.SemaphoreType.DMA((4, 2, 6)),
            pltpu.SemaphoreType.DMA((4, 2, 6)),
        ],
        compiler_params=pltpu.CompilerParams(
            collective_id=0, has_side_effects=True, vmem_limit_bytes=62 * 1024 * 1024
        ),
    )(
        state, weights, drive, leak, link_dev, link_blk, offsets, gram_prev,
    )


def finish_gram(last, gram_part):
    rows = last.shape[0]
    state, gram_prev = last, gram_part
    anywhere = pl.BlockSpec(memory_space=pl.ANY)
    return pl.pallas_call(
        functools.partial(closing, last.shape[2] // 2),
        out_shape=(
            jax.ShapeDtypeStruct(state.shape, state.dtype),
            jax.ShapeDtypeStruct(gram_prev.shape, gram_prev.dtype),
        ),
        in_specs=[anywhere, anywhere],
        out_specs=(anywhere, anywhere),
        scratch_shapes=[
            pltpu.VMEM(state.shape, state.dtype),
            pltpu.VMEM(gram_prev.shape, gram_prev.dtype),
            *[pltpu.SemaphoreType.DMA((rows,))] * 4,
        ],
        compiler_params=pltpu.CompilerParams(vmem_limit_bytes=62 * 1024 * 1024),
    )(last, gram_part)


def listed(n_gy, level, peer, spot, pick, state, weights, drive, leak, link_dev, link_blk, offsets, gram_prev):
    rows, cols, seq, units = state.shape
    blocks = rows * cols
    anywhere = pl.BlockSpec(memory_space=pl.ANY)
    scalars = pl.BlockSpec(memory_space=pltpu.SMEM)
    slots, first = LEVELS[level]
    block = (seq // 2, units)
    held = lambda *n: pltpu.VMEM((*n, *block), jnp.bfloat16)
    copies = pltpu.SemaphoreType.DMA
    return pl.pallas_call(
        functools.partial(routed, n_gy, level),
        out_shape=(
            jax.ShapeDtypeStruct(state.shape, state.dtype),
            jax.ShapeDtypeStruct(gram_prev.shape, gram_prev.dtype),
        ),
        in_specs=[
            anywhere, anywhere, anywhere, anywhere, pl.BlockSpec(memory_space=pltpu.VMEM),
            scalars, scalars, scalars, scalars, scalars, anywhere,
        ],
        out_specs=(anywhere, anywhere),
        scratch_shapes=[
            *[held(2 * blocks)] * 4,
            *[held(2 * blocks + 4 * SLOTS)] * 4,
            *[held(AHEAD)] * 8,
            held(4, 2, first), held(4, 2, slots - first), held(4, 2, rows + 2), held(4, 2, 2),
            held(rows, cols + 2), held(3, cols + 2), held(3, cols + 2),
            pltpu.VMEM(weights.shape, weights.dtype),
            pltpu.VMEM(drive.shape, drive.dtype),
            pltpu.VMEM(gram_prev.shape, gram_prev.dtype),
            pltpu.VMEM((blocks, *block), jnp.float32),
            pltpu.VMEM((blocks, seq, units), jnp.bfloat16),
            copies((6 + rows,)), copies((1 + rows,)), copies((4, 3)),
            *[copies((4, 2, 3))] * 4,
            *[copies((2, rows))] * 2,
            *[copies((4, 2, rows + 2))] * 2,
        ],
        compiler_params=pltpu.CompilerParams(
            collective_id=2 + level, has_side_effects=True, vmem_limit_bytes=62 * 1024 * 1024
        ),
    )(
        state.reshape(blocks, seq, units), peer, weights, drive, leak, spot, pick,
        link_dev, link_blk, offsets, gram_prev,
    )


def fast_shards(n_gy, state, weights, drive, leak, link_dev, link_blk, offsets, gram_prev):
    rows, cols, seq, units = state.shape
    blocks = rows * cols
    anywhere = pl.BlockSpec(memory_space=pl.ANY)
    vector = pl.BlockSpec(memory_space=pltpu.VMEM)
    scalars = pl.BlockSpec(memory_space=pltpu.SMEM)
    ldev, lblk = link_dev.transpose(0, 3, 1, 2), link_blk.transpose(0, 3, 1, 2)
    table = lambda *n: jax.ShapeDtypeStruct((*n, 128), jnp.int32)
    spot, pick, verdict, peer = pl.pallas_call(
        functools.partial(agree, n_gy),
        out_shape=(
            table(8), table(len(LEVELS), 32), jax.ShapeDtypeStruct((1, 1), jnp.int32),
            jax.ShapeDtypeStruct((blocks, seq, units), state.dtype),
        ),
        in_specs=[scalars, scalars, anywhere],
        out_specs=(vector, vector, scalars, anywhere),
        scratch_shapes=[
            pltpu.VMEM((n_gy, 8, 128), jnp.int32),
            pltpu.SemaphoreType.DMA((n_gy,)),
            pltpu.SemaphoreType.DMA((n_gy,)),
        ],
        compiler_params=pltpu.CompilerParams(collective_id=1, has_side_effects=True),
    )(ldev, lblk, state.reshape(blocks, seq, units))
    operands = (state, weights, drive, leak.transpose(1, 0, 2), ldev, lblk, offsets.T, gram_prev)
    branches = [lambda: general(n_gy, *operands)]
    for level in range(len(LEVELS)):
        branches.append(functools.partial(listed, n_gy, level, peer, spot, pick, *operands))
    last, gram = lax.switch(verdict.reshape(()), branches)
    return finish_gram(last, gram)


def solution(mesh):
    part = shards
    if mesh.shape["gx"] == 8:
        part = functools.partial(fast_shards, mesh.shape["gy"])
    return jax.shard_map(
        part,
        mesh=mesh,
        in_specs=(
            P("gx", "gy", None, None),
            P("gx", "gy", None, None, None),
            P(None, "gx", "gy", None, None),
            P("gx", "gy", None),
            P(None, "gy", None, None),
            P(None, "gy", None, None),
            P(),
            P("gx", "gy", None, None),
        ),
        out_specs=(P("gx", "gy", None, None), P("gx", "gy", None, None)),
        check_vma=False,
    )
```

```python
import functools

import jax
import jax.numpy as jnp
from jax import lax
from jax.experimental import pallas as pl
from jax.experimental.pallas import tpu as pltpu
from jax.sharding import PartitionSpec as P

MESH = pl.DeviceIdType.MESH
PART, ALONG_X, ALONG_Y, X_PART, Y_PART, DIAG, D_PART = range(7)


def padded(x, sides, width):
    for axis, dim in sides:
        size, length = (lax.axis_size(axis), x.shape[dim])
        up = [(i, (i + 1) % size) for i in range(size - 1)]
        down = [(j, i) for i, j in up]
        last = lax.slice_in_dim(x, length - width, length, axis=dim)
        first = lax.slice_in_dim(x, 0, width, axis=dim)
        before = lax.ppermute(last, axis, up)
        after = lax.ppermute(first, axis, down)
        x = jnp.concatenate([before, x, after], axis=dim)
    return x


def shards(state, weights, drive, leak, link_dev, link_blk, offsets, gram_prev):
    grid_rows, grid_cols, batch_cols, units = state.shape
    nblocks = grid_rows * grid_cols
    nlinks = link_dev.shape[-1]
    nstencil = offsets.shape[0]
    gx_size = lax.axis_size("gx")
    own_index = lax.axis_index("gx")
    all_dev = link_dev[:, 0].reshape(gx_size, nblocks * nlinks)
    all_blk = link_blk[:, 0].reshape(gx_size, nblocks * nlinks)
    my_dev = lax.dynamic_index_in_dim(all_dev, own_index, 0, keepdims=False)
    my_blk = lax.dynamic_index_in_dim(all_blk, own_index, 0, keepdims=False)
    w_long = weights[:, :, nstencil : nstencil + nlinks].reshape(nblocks, nlinks, units, units)
    current = state
    gram = gram_prev
    for step_id in range(drive.shape[0]):
        extended = padded(current, (("gx", 0), ("gy", 1)), 1)
        preact = jnp.zeros((grid_rows, grid_cols, batch_cols, units), jnp.float32)
        for offset_id in range(nstencil):
            zero = jnp.zeros((), jnp.int32)
            start_r = 1 + offsets[offset_id, 0]
            start_c = 1 + offsets[offset_id, 1]
            nearby = lax.dynamic_slice(
                extended, (start_r, start_c, zero, zero), (grid_rows, grid_cols, batch_cols, units)
            )
            preact = preact + jnp.einsum(
                "rcsu,rcuv->rcsv",
                nearby,
                weights[:, :, offset_id],
                preferred_element_type=jnp.float32,
            )
        flat_state = current.reshape(nblocks, batch_cols, units)
        whole = lax.all_gather(flat_state[None], "gx", axis=0, tiled=True)
        picked = whole.reshape(gx_size * nblocks, batch_cols, units)[my_dev * nblocks + my_blk]
        picked = picked.reshape(nblocks, nlinks, batch_cols, units)
        distant = jnp.einsum("blsu,bluv->bsv", picked, w_long, preferred_element_type=jnp.float32)
        preact = preact + distant.reshape(grid_rows, grid_cols, batch_cols, units)
        preact = preact + jnp.einsum(
            "rcsu,rcuv->rcsv",
            drive[step_id],
            weights[:, :, nstencil + nlinks],
            preferred_element_type=jnp.float32,
        )
        rate = leak[:, :, None, :]
        current = ((1.0 - rate) * current.astype(jnp.float32) + rate * jnp.tanh(preact)).astype(
            jnp.bfloat16
        )
        gram = gram + jnp.einsum(
            "rcsu,rcsv->rcuv", current, current, preferred_element_type=jnp.float32
        )
    return (current, gram)


def reservoir(
    n_gy, state, w, drive, leak, ldev, lblk, offs, gprev, out, gout,
    gath00, gath01, gath10, gath11, ext00, ext01, ext10, ext11, wv, dv, gv, acc, xf,
    load_sem, store_sem, send_sem, recv_sem, zsend_sem, zrecv_sem,
):
    rows, cols, seq, units = state.shape
    nstencil, nlinks = offs.shape[1], ldev.shape[1]
    half = seq // 2
    g, b = lax.axis_index("gx"), lax.axis_index("gy")
    core, x, y = lax.rem(g, 2), lax.rem(lax.div(g, 2), 2), lax.div(g, 4)
    near = lambda fy, fx, fc: (
        (1 - y if fy else y) * 4 + (1 - x if fx else x) * 2 + (1 - core if fc else core)
    )
    ids = {
        PART: near(0, 0, 1), ALONG_X: near(0, 1, 0), ALONG_Y: near(1, 0, 0),
        X_PART: near(0, 1, 1), Y_PART: near(1, 0, 1), DIAG: near(1, 1, 0), D_PART: near(1, 1, 1),
    }
    has_left, has_right = b > 0, b < n_gy - 1
    has_up, has_down = g > 0, g < 7
    gaths, exts = (gath00, gath01, gath10, gath11), (ext00, ext01, ext10, ext11)

    loads = []

    def load(src, dst):
        copy = pltpu.make_async_copy(src, dst, load_sem.at[len(loads)])
        copy.start()
        loads.append(copy)
        return copy

    for r in range(rows):
        for s in (0, 1):
            load(state.at[r, :, pl.ds(s * half, half)], gaths[s].at[g, pl.ds(r * cols, cols)])

    barrier = pltpu.get_barrier_semaphore()
    for rel in (PART, ALONG_X, ALONG_Y):
        pl.semaphore_signal(barrier, inc=1, device_id={"gx": ids[rel]}, device_id_type=MESH)

    @pl.when(has_left)
    def _():
        pl.semaphore_signal(barrier, inc=1, device_id={"gy": b - 1}, device_id_type=MESH)

    @pl.when(has_right)
    def _():
        pl.semaphore_signal(barrier, inc=1, device_id={"gy": b + 1}, device_id_type=MESH)

    inside = jnp.logical_and(has_left, has_right)

    @pl.when(inside)
    def _():
        pl.semaphore_wait(barrier, 5)

    @pl.when(jnp.logical_not(inside))
    def _():
        pl.semaphore_wait(barrier, 4 if n_gy > 1 else 3)

    sends = []

    def send(t, rel_from, r, to, rel_there):
        origin = g if rel_from is None else ids[rel_from]
        here = gaths[t].at[origin, pl.ds(r * cols, cols)]
        src = state.at[r, :, pl.ds(t * half, half)] if rel_from is None and t < 2 else here
        copy = pltpu.make_async_remote_copy(
            src_ref=src, dst_ref=here,
            send_sem=send_sem.at[len(sends)], recv_sem=recv_sem.at[t, rel_there, r],
            device_id={"gx": ids[to]}, device_id_type=MESH,
        )
        copy.start()
        sends.append(copy)

    def send_own(t, r, to):
        send(t, None, r, to, to)

    def arrived(t, rel, r):
        here = gaths[t].at[ids[rel], pl.ds(r * cols, cols)]
        pltpu.make_async_remote_copy(
            src_ref=here, dst_ref=here,
            send_sem=send_sem.at[0], recv_sem=recv_sem.at[t, rel, r],
            device_id={"gx": ids[PART]}, device_id_type=MESH,
        ).wait_recv()

    def relay(t, rel, r, across=None):
        arrived(t, rel, r)
        if across is not None:
            send(t, rel, r, across, DIAG)
        send(t, rel, r, PART, {ALONG_X: X_PART, ALONG_Y: Y_PART, DIAG: D_PART}[rel])

    def rim_copy(t, side, kind):
        col = 0 if side == 0 else cols - 1
        there = cols + 1 if side == 0 else 0
        gath, ext = gaths[t], exts[t]
        if kind == 0:
            return [
                pltpu.make_async_remote_copy(
                    src_ref=state.at[r, col, pl.ds(t * half, half)]
                    if t < 2
                    else gath.at[g, r * cols + col],
                    dst_ref=ext.at[r + 1, there],
                    send_sem=zsend_sem.at[t, side, r], recv_sem=zrecv_sem.at[t, side, r],
                    device_id={"gy": b - 1 if side == 0 else b + 1}, device_id_type=MESH,
                )
                for r in range(rows)
            ]
        src = (
            gath.at[lax.rem(g + 7, 8), (rows - 1) * cols + col]
            if kind == 1
            else gath.at[lax.rem(g + 1, 8), col]
        )
        return [
            pltpu.make_async_remote_copy(
                src_ref=src,
                dst_ref=ext.at[0 if kind == 1 else rows + 1, there],
                send_sem=zsend_sem.at[t, side, rows + kind - 1],
                recv_sem=zrecv_sem.at[t, side, rows + kind - 1],
                device_id={"gy": b - 1 if side == 0 else b + 1}, device_id_type=MESH,
            )
        ]

    def rims(t, do, kinds):
        for side in (0, 1):
            present = (has_left, has_right)
            who = present[side] if do != "wait_recv" else present[1 - side]
            for kind in kinds:
                cond = who
                if kind == 1:
                    cond = jnp.logical_and(who, has_up)
                if kind == 2:
                    cond = jnp.logical_and(who, has_down)

                @pl.when(cond)
                def _():
                    for copy in rim_copy(t, side, kind):
                        getattr(copy, do)()

    def begin(t, r):
        if r != 2:
            send_own(t, r, ALONG_X)
        if r != 1:
            send_own(t, r, ALONG_Y)
        send_own(t, r, PART)

    def exchange(t):
        relay(t, ALONG_X, 0, ALONG_Y)
        send_own(t, 1, ALONG_Y)
        relay(t, ALONG_Y, 0)
        relay(t, ALONG_X, 3)
        relay(t, ALONG_Y, 3, ALONG_X)
        send_own(t, 2, ALONG_X)
        relay(t, ALONG_X, 1, ALONG_Y)
        relay(t, ALONG_Y, 2, ALONG_X)

    def borders(t):
        relay(t, DIAG, 0)
        relay(t, DIAG, 3)
        for rel in (PART, X_PART, D_PART):
            arrived(t, rel, 0)
            arrived(t, rel, 3)
        rims(t, "start", (1, 2))
        fill(t)
        rims(t, "wait_recv", (0, 1, 2))

    def finish(t):
        relay(t, ALONG_Y, 1)
        relay(t, ALONG_X, 2)
        relay(t, DIAG, 1)
        relay(t, DIAG, 2)
        for rel in (PART, X_PART, D_PART):
            arrived(t, rel, 1)
            arrived(t, rel, 2)
        for r in range(rows):
            arrived(t, Y_PART, r)

    def fill(t):
        gath, ext = gaths[t], exts[t]

        def place(i, carry):
            r, c = i // cols, lax.rem(i, cols)
            ext[r + 1, c + 1] = gath[g, i]
            return carry

        lax.fori_loop(0, rows * cols, place, 0)
        zero = jnp.zeros((half, units), jnp.bfloat16)

        @pl.when(has_up)
        def _():
            for c in range(cols):
                ext[0, c + 1] = gath[lax.rem(g + 7, 8), (rows - 1) * cols + c]

        @pl.when(has_down)
        def _():
            for c in range(cols):
                ext[rows + 1, c + 1] = gath[lax.rem(g + 1, 8), c]

        for there, edge in ((0, has_up), (rows + 1, has_down)):

            @pl.when(jnp.logical_not(edge))
            def _():
                for c in range(cols + 2):
                    ext[there, c] = zero

        for there, side in ((0, has_left), (cols + 1, has_right)):

            @pl.when(jnp.logical_not(side))
            def _():
                for r in range(rows):
                    ext[r + 1, there] = zero
                for r, edge in ((0, has_up), (rows + 1, has_down)):

                    @pl.when(edge)
                    def _():
                        ext[r, there] = zero

    def dot(a, weight):
        return jnp.dot(a, weight, preferred_element_type=jnp.float32)

    def nearby(t):
        ext = exts[t]

        def one(i, carry):
            r, c = i // cols, lax.rem(i, cols)
            total = dot(
                dv[t // 2, r, c, pl.ds(t % 2 * half, half)], wv[r, c, nstencil + nlinks]
            )
            for k in range(nstencil):
                total = total + dot(ext[r + 1 + offs[0, k], c + 1 + offs[1, k]], wv[r, c, k])
            acc[i] = total
            return carry

        lax.fori_loop(0, rows * cols, one, 0)

    def gram_of(r, c, now):
        gv[r, c] += lax.dot_general(
            now, now, (((0,), (0,)), ((), ())), preferred_element_type=jnp.float32
        )

    def distant(t, r):
        gath = gaths[t]

        def one(c, carry):
            i = r * cols + c
            total = acc[i]
            for l in range(nlinks):
                total = total + dot(gath[ldev[g, l, 0, i], lblk[g, l, 0, i]], wv[r, c, nstencil + l])
            rate = leak[c, pl.ds(r, 1), :]
            old = gath[g, i].astype(jnp.float32)
            now = ((1.0 - rate) * old + rate * jnp.tanh(total)).astype(jnp.bfloat16)
            if t >= 2:
                xf[i, pl.ds((t - 2) * half, half)] = now
            else:
                gaths[t + 2][g, i] = now
            if t < 3:
                gram_of(r, c, now)
            return carry

        lax.fori_loop(0, cols, one, 0)

    order = (0, 3, 1, 2)

    def start(t):
        for r in order:
            begin(t, r)
        rims(t, "start", (0,))

    stores = []

    def store(src, dst):
        copy = pltpu.make_async_copy(src, dst, store_sem.at[len(stores)])
        copy.start()
        stores.append(copy)

    start(0)
    for r in range(rows):
        load(w.at[r], wv.at[r])
    load(drive, dv)
    load(gprev, gv)
    for t in range(4):
        exchange(t)
        if t < 3:
            start(t + 1)
        if t == 0:
            for copy in loads:
                copy.wait()
        borders(t)
        nearby(t)
        finish(t)
        for r in range(rows):
            distant(t, r)
            if t == 3:
                store(xf.at[pl.ds(r * cols, cols)], out.at[r])
        if t == 2:
            store(gv, gout)
    for copy in sends:
        copy.wait_send()
    for t in range(4):
        rims(t, "wait_send", (0, 1, 2))
    for copy in stores:
        copy.wait()


def closing(half, x, gram, out, gout, xv, gv, x_sem, g_sem, out_sem, gout_sem):
    rows, cols = x.shape[:2]
    copy = pltpu.make_async_copy
    x_in = [copy(x.at[r], xv.at[r], x_sem.at[r]) for r in range(rows)]
    g_in = [copy(gram.at[r], gv.at[r], g_sem.at[r]) for r in range(rows)]
    x_out = [copy(xv.at[r], out.at[r], out_sem.at[r]) for r in range(rows)]
    g_out = [copy(gv.at[r], gout.at[r], gout_sem.at[r]) for r in range(rows)]
    for r in range(rows):
        x_in[r].start()
        g_in[r].start()
    for r in range(rows):
        x_in[r].wait()
        x_out[r].start()
        g_in[r].wait()
        for c in range(cols):
            now = xv[r, c, pl.ds(half, half)]
            gv[r, c] += lax.dot_general(
                now, now, (((0,), (0,)), ((), ())), preferred_element_type=jnp.float32
            )
        g_out[r].start()
    for r in range(rows):
        x_out[r].wait()
        g_out[r].wait()


LEVELS = ((13, 8), (12, 7))
SLOTS, AHEAD = 13, 5
LANES = 16


def route(ldev, lblk, spot, pick):
    rows_of = lambda n: lax.broadcasted_iota(jnp.int32, (n, 128), 0)
    lanes_of = lambda n: lax.broadcasted_iota(jnp.int32, (n, 128), 1)
    nlinks, nblocks = ldev.shape[1], ldev.shape[3]
    g = lax.axis_index("gx")
    core, home = g % 2, g // 2
    lane = lanes_of(8)
    chip, block = lane // 32, lane % LANES

    needs = []
    for c in range(4):
        need = jnp.zeros((8, 128), jnp.bool_)
        for a in (2 * c, 2 * c + 1):
            for l in range(nlinks):
                for q in range(nblocks):
                    need = need | (lane == ldev[a, l, 0, q] * LANES + lblk[a, l, 0, q])
        for src, dst in ((2 * c - 1, 2 * c), (2 * c + 2, 2 * c + 1)):
            if 0 <= src < 8:
                first = nblocks - 3 if src < dst else 0
                need = need | ((lane >= src * LANES + first) & (lane < src * LANES + first + 3))
        needs.append(need.astype(jnp.int32))

    def seen(flip):
        return jnp.where(
            chip == 0, needs[flip],
            jnp.where(chip == 1, needs[1 ^ flip], jnp.where(chip == 2, needs[2 ^ flip], needs[3 ^ flip])),
        )

    nx, ny, nd = seen(1), seen(2), seen(3)
    only_x, both, neither, only_y = nd * nx * (1 - ny), nd * nx * ny, nd * (1 - nx) * (1 - ny), nd * ny * (1 - nx)
    classes = [only_x, both, neither, only_y, nx, ny]

    def stack(parts):
        sub, stacked = rows_of(8), jnp.zeros((8, 128), jnp.int32)
        for k, part in enumerate(parts):
            stacked = jnp.where(sub == k, part, stacked)
        return stacked.astype(jnp.float32)

    def times(x, matrix):
        return jnp.dot(
            x.astype(jnp.bfloat16), matrix.astype(jnp.float32).astype(jnp.bfloat16),
            preferred_element_type=jnp.float32,
        ).astype(jnp.int32)

    above, across = rows_of(128), lanes_of(128)
    upto = (above <= across) & (above // 32 == across // 32)
    counted = stack(classes)
    sums = times(counted, upto)
    totals = [times(counted, above // 32 == c) for c in range(4)]
    row = lambda x, k: jnp.broadcast_to(x[k : k + 1], (8, 128))

    cand = rows_of(32) * 128 + lanes_of(32)
    wide = lambda c, k: jnp.broadcast_to(totals[c][k : k + 1], (32, 128))
    fx, fy, rx, ry = [], [], [], []

    def passed(counts, digit):
        total = counts[0] + counts[1] + counts[2] + counts[3]
        start = (2 * counts[0] + counts[1] + counts[2] + 1) // 2 - 4
        return total, jnp.maximum(jnp.minimum(start + digit, total), 0)

    for c in range(4):
        counts = [wide(c, k) for k in range(6)]
        total, m = passed(counts, (cand >> (3 * c)) & 7)
        rest = total - m
        rx.append(m)
        ry.append(rest)
        fx.append(counts[4] + jnp.maximum(m - counts[0] - counts[1], 0))
        fy.append(
            counts[5] + jnp.maximum(jnp.minimum(rest - counts[3], counts[2]), 0)
            + jnp.maximum(rest - counts[3] - counts[2] - counts[1], 0)
        )
    worst = jnp.zeros((32, 128), jnp.int32)
    for c in range(4):
        worst = jnp.maximum(worst, fx[c] + ry[c ^ 2])
        worst = jnp.maximum(worst, fy[c] + rx[c ^ 1])
        worst = jnp.where(jnp.maximum(rx[c], ry[c]) > 2 * AHEAD, 255, worst)
    best = jnp.min(worst * 4096 + cand)

    pickc = lambda values: jnp.where(
        chip == 0, values[0], jnp.where(chip == 1, values[1], jnp.where(chip == 2, values[2], values[3]))
    )
    count = [pickc([row(totals[c], k) for c in range(4)]) for k in range(6)]
    digit = pickc([(best >> (3 * c)) & 7 for c in range(4)])
    total, m = passed(count, digit)
    rank = jnp.where(
        only_x > 0, row(sums, 0) - 1,
        jnp.where(
            both > 0, count[0] + row(sums, 1) - 1,
            jnp.where(
                neither > 0, count[0] + count[1] + row(sums, 2) - 1,
                count[0] + count[1] + count[2] + row(sums, 3) - 1,
            ),
        ),
    )
    via_x = jnp.where(rank < m, nd, 0)
    via_y = nd - via_x
    more = times(stack([nx * (1 - via_x), ny * (1 - via_y)]), upto)
    over = rank - m
    pos_x = jnp.where(via_x > 0, rank, m + row(more, 0) - 1)
    pos_y = jnp.where(via_y > 0, over, total - m + row(more, 1) - 1)
    held_x, held_y = jnp.maximum(nx, via_x), jnp.maximum(ny, via_y)

    mine = block + jnp.where((lane // LANES) % 2 == core, 0, 12)
    base = 2 * nblocks
    inward = lambda link, k, p: base + 2 * SLOTS * link + jnp.where(k == core, 0, SLOTS) + p
    odd = lambda x: x & 1
    where_to = lambda slots: jnp.where(
        chip == home, mine,
        jnp.where(
            chip == (home ^ 1), inward(0, odd(pos_x), pos_x >> 1),
            jnp.where(
                chip == (home ^ 2), inward(1, odd(pos_y + 1), pos_y >> 1),
                jnp.where(
                    via_x > 0, inward(1, odd(rank), slots - 1 - (rank >> 1)),
                    inward(0, odd(over + 1), slots - 1 - (over >> 1)),
                ),
            ),
        ),
    )
    there = where_to(LEVELS[0][0])
    for n, (slots, _) in enumerate(LEVELS):
        there = jnp.where(rows_of(8) == n, where_to(slots), there)
    spot[...] = jnp.maximum(jnp.minimum(there, base + 4 * SLOTS - 1), 0)

    sub = rows_of(32)
    place, is_y = sub % 16, sub >= 16
    full = lambda x: jnp.broadcast_to(x[0:1], (32, 128))
    own_chip = full(jnp.where(chip == home, 1, 0)) > 0
    own_at = jnp.where(is_y, full(pos_y), full(pos_x))
    own_core = jnp.where(is_y, odd(own_at + 1), odd(own_at))
    own_held = jnp.where(is_y, full(held_y), full(held_x)) > 0
    own_hit = own_chip & own_held & (own_at >> 1 == place) & (own_core == core)
    pass_x = full(jnp.where(chip == (home ^ 2), via_y, 0))
    pass_y = full(jnp.where(chip == (home ^ 1), via_x, 0))
    pass_held = jnp.where(is_y, pass_y, pass_x) > 0
    pass_rank = jnp.where(is_y, full(rank), full(over))
    pass_core = jnp.where(is_y, odd(pass_rank), odd(pass_rank + 1))
    for n, (slots, first) in enumerate(LEVELS):
        pass_hit = pass_held & (slots - 1 - (pass_rank >> 1) == place) & (pass_core == core)
        value = jnp.where(own_hit, full(mine), 0) + jnp.where(pass_hit, base + (pass_rank >> 1), 0)
        value = jnp.sum(value.astype(jnp.float32), axis=1, keepdims=True).astype(jnp.int32)
        value = jnp.broadcast_to(value, (32, 128))
        most = jnp.where(place < first, base - 1, base + AHEAD - 1)
        pick[n] = jnp.maximum(jnp.minimum(value, most), 0)
    least = jnp.zeros((8, 128), jnp.int32) + (best >> 12)
    level = jnp.zeros((8, 128), jnp.int32)
    for n, (slots, _) in enumerate(LEVELS):
        level = jnp.where(least <= 2 * slots, n + 1, level)
    return level


def agree(n_gy, ldev, lblk, state, spot, pick, verdict, peer, votes, send_sem, recv_sem):
    g, b = lax.axis_index("gx"), lax.axis_index("gy")
    part = g + 1 - 2 * lax.rem(g, 2)
    barrier = pltpu.get_barrier_semaphore()
    pl.semaphore_signal(barrier, inc=1, device_id={"gx": part}, device_id_type=MESH)
    for d in range(1, n_gy):
        pl.semaphore_signal(barrier, inc=1, device_id={"gy": lax.rem(b + d, n_gy)}, device_id_type=MESH)
    votes[0] = route(ldev, lblk, spot, pick)
    pl.semaphore_wait(barrier, n_gy)
    copies = []
    for d in range(1, n_gy):
        copies.append(pltpu.make_async_remote_copy(
            src_ref=votes.at[0], dst_ref=votes.at[d], send_sem=send_sem.at[d], recv_sem=recv_sem.at[d],
            device_id={"gy": lax.rem(b + d, n_gy)}, device_id_type=MESH,
        ))
    copies.append(pltpu.make_async_remote_copy(
        src_ref=state, dst_ref=peer, send_sem=send_sem.at[0], recv_sem=recv_sem.at[0],
        device_id={"gx": part}, device_id_type=MESH,
    ))
    for copy in copies:
        copy.start()
    for copy in copies:
        copy.wait()
    verdict[0, 0] = jnp.min(jnp.min(votes[...], axis=0))


def routed(
    n_gy, level, state, peer, w, drive, leak, spot, pick, ldev, lblk, offs, gprev, out, gout,
    own0, own1, own2, own3, gath0, gath1, gath2, gath3,
    headx0, headx1, headx2, headx3, heady0, heady1, heady2, heady3,
    early, late, side, corner, mid, top, bot, wv, dv, gv, acc, xf,
    load_sem, store_sem, local_sem, link_send, link_recv, pass_send, pass_recv, peer_send, peer_recv,
    zsend_sem, zrecv_sem,
):
    slots, first = LEVELS[level]
    seq, units = state.shape[1:]
    rows, cols = w.shape[:2]
    blocks = rows * cols
    nstencil, nlinks = offs.shape[1], ldev.shape[1]
    half = seq // 2
    base = 2 * blocks
    g, b = lax.axis_index("gx"), lax.axis_index("gy")
    core, x, y = lax.rem(g, 2), lax.rem(lax.div(g, 2), 2), lax.div(g, 4)
    part = y * 4 + x * 2 + 1 - core
    along = (y * 4 + (1 - x) * 2 + core, (1 - y) * 4 + x * 2 + core)
    has_left, has_right = b > 0, b < n_gy - 1
    has_up, has_down = g > 0, g < 7
    owns, gaths = (own0, own1, own2, own3), (gath0, gath1, gath2, gath3)
    heads = ((headx0, headx1, headx2, headx3), (heady0, heady1, heady2, heady3))

    def local(src, dst, sem):
        copy = pltpu.make_async_copy(src, dst, sem)
        copy.start()
        return copy

    firsts = []
    for t in (0, 1):
        firsts.append([
            local(state.at[:, pl.ds(t * half, half)], owns[t].at[pl.ds(0, blocks)], load_sem.at[2 * t]),
            local(peer.at[:, pl.ds(t * half, half)], owns[t].at[pl.ds(blocks, blocks)], load_sem.at[2 * t + 1]),
        ])

    barrier = pltpu.get_barrier_semaphore()
    for to in (part, *along):
        pl.semaphore_signal(barrier, inc=1, device_id={"gx": to}, device_id_type=MESH)

    @pl.when(has_left)
    def _():
        pl.semaphore_signal(barrier, inc=1, device_id={"gy": b - 1}, device_id_type=MESH)

    @pl.when(has_right)
    def _():
        pl.semaphore_signal(barrier, inc=1, device_id={"gy": b + 1}, device_id_type=MESH)

    inside = jnp.logical_and(has_left, has_right)

    @pl.when(inside)
    def _():
        pl.semaphore_wait(barrier, 5)

    @pl.when(jnp.logical_not(inside))
    def _():
        pl.semaphore_wait(barrier, 4 if n_gy > 1 else 3)

    bounds = ((0, AHEAD), (AHEAD, first), (first, slots))

    def region(t, link, lead, part_id):
        low, high = bounds[part_id]
        return gaths[t].at[pl.ds(base + 2 * SLOTS * link + (0 if lead else SLOTS) + low, high - low)]

    def link_copy(t, link, part_id):
        low, high = bounds[part_id]
        src = late.at[t, link] if part_id == 2 else early.at[t, link, pl.ds(low, high - low)]
        dst = heads[link][t] if part_id == 0 else region(t, link, True, part_id)
        return pltpu.make_async_remote_copy(
            src_ref=src, dst_ref=dst, send_sem=link_send.at[t, link, part_id], recv_sem=link_recv.at[t, link, part_id],
            device_id={"gx": along[link]}, device_id_type=MESH,
        )

    def pass_copy(t, link, part_id):
        src = heads[link][t] if part_id == 0 else region(t, link, True, part_id)
        return pltpu.make_async_remote_copy(
            src_ref=src, dst_ref=region(t, link, False, part_id),
            send_sem=pass_send.at[t, link, part_id], recv_sem=pass_recv.at[t, link, part_id],
            device_id={"gx": part}, device_id_type=MESH,
        )

    def head_copy(t, link):
        return pltpu.make_async_copy(heads[link][t], region(t, link, True, 0), local_sem.at[t, link])

    def own_copy(t):
        return pltpu.make_async_copy(owns[t], gaths[t].at[pl.ds(0, base)], local_sem.at[t, 2])

    def peer_copy(t, r):
        return pltpu.make_async_remote_copy(
            src_ref=owns[t].at[pl.ds(r * cols, cols)], dst_ref=owns[t].at[pl.ds(blocks + r * cols, cols)],
            send_sem=peer_send.at[t - 2, r], recv_sem=peer_recv.at[t - 2, r],
            device_id={"gx": part}, device_id_type=MESH,
        )

    def rim_copy(t, to, r):
        src = owns[t].at[r * cols + (0 if to == 0 else cols - 1)] if r < rows else corner.at[t, to, r - rows]
        return pltpu.make_async_remote_copy(
            src_ref=src, dst_ref=side.at[t, 1 - to, r],
            send_sem=zsend_sem.at[t, to, r], recv_sem=zrecv_sem.at[t, 1 - to, r],
            device_id={"gy": b - 1 if to == 0 else b + 1}, device_id_type=MESH,
        )

    def rim_wait(t, came, r):
        pltpu.make_async_remote_copy(
            src_ref=side.at[t, came, r], dst_ref=side.at[t, came, r],
            send_sem=zsend_sem.at[t, came, r], recv_sem=zrecv_sem.at[t, came, r],
            device_id={"gy": b - 1 if came == 0 else b + 1}, device_id_type=MESH,
        ).wait_recv()

    def rims(t, do, corners):
        for s, present in ((0, has_left), (1, has_right)):
            for r in ((rows, rows + 1) if corners else range(rows)):
                cond = present
                if corners:
                    cond = jnp.logical_and(present, has_up if r == rows else has_down)

                @pl.when(cond)
                def _():
                    do(t, s, r)

    def begin(t):
        for j in range(first):
            for link in (0, 1):
                early[t, link, j] = owns[t][pick[level, 16 * link + j, 0]]
            if j == AHEAD - 1:
                for link in (0, 1):
                    link_copy(t, link, 0).start()
        for link in (0, 1):
            link_copy(t, link, 1).start()
        rims(t, lambda *at: rim_copy(*at).start(), False)
        own_copy(t).start()

    def follow(t):
        for link in (0, 1):
            link_copy(t, link, 0).wait_recv()
        for link in (0, 1):
            for j in range(slots - first):
                at = pick[level, 16 * link + first + j, 0]
                passing = at >= base
                one = owns[t][jnp.where(passing, 0, at)]
                two = heads[1 - link][t][jnp.where(passing, at - base, 0)]
                late[t, link, j] = jnp.where(passing, two, one)
            link_copy(t, link, 2).start()
        for link in (0, 1):
            pass_copy(t, link, 0).start()
            head_copy(t, link).start()

    def relay(t, part_id):
        for link in (0, 1):
            link_copy(t, link, part_id).wait_recv()
            pass_copy(t, link, part_id).start()

    def settle(t):
        own_copy(t).wait()
        for link in (0, 1):
            head_copy(t, link).wait()
            for part_id in range(3):
                pass_copy(t, link, part_id).wait_recv()

    def dot(a, weight):
        return jnp.dot(a, weight, preferred_element_type=jnp.float32)

    def clear():
        zero = jnp.zeros((half, units), jnp.bfloat16)

        @pl.when(jnp.logical_not(has_up))
        def _():
            for c in range(cols + 2):
                top[0, c] = zero

        @pl.when(jnp.logical_not(has_down))
        def _():
            for c in range(cols + 2):
                bot[2, c] = zero

        for at, present in ((0, has_left), (cols + 1, has_right)):

            @pl.when(jnp.logical_not(present))
            def _():
                for r in range(rows):
                    mid[r, at] = zero
                for r in range(3):
                    top[r, at] = zero
                    bot[r, at] = zero

    def put(r, at, value):
        mid[r, at] = value
        if r < 2:
            top[r + 1, at] = value
        if r >= rows - 2:
            bot[r - rows + 2, at] = value

    def fill_mid(t):
        for r in range(rows):
            for c in range(cols):
                put(r, c + 1, owns[t][r * cols + c])
        for s, present in ((0, has_left), (1, has_right)):

            @pl.when(present)
            def _():
                for r in range(rows):
                    put(r, 0 if s == 0 else cols + 1, side[t, s, r])

    def fill_rims(t):
        gath = gaths[t]
        for up, present in ((True, has_up), (False, has_down)):

            @pl.when(present)
            def _():
                for c in range(cols):
                    src = (g - 1) * LANES + (rows - 1) * cols + c if up else (g + 1) * LANES + c
                    value = gath[spot[level, src]]
                    if up:
                        top[0, c + 1] = value
                    else:
                        bot[2, c + 1] = value
                    for to, col in ((0, 0), (1, cols - 1)):
                        if c == col:
                            corner[t, to, 0 if up else 1] = value

    def fill_corners(t):
        for s, has in ((0, has_left), (1, has_right)):
            at = 0 if s == 0 else cols + 1

            @pl.when(jnp.logical_and(has, has_up))
            def _():
                top[0, at] = side[t, s, rows]

            @pl.when(jnp.logical_and(has, has_down))
            def _():
                bot[2, at] = side[t, s, rows + 1]

    def over(r, body):
        def one(c, carry):
            body(c, r * cols + c)
            return carry

        lax.fori_loop(0, cols, one, 0)

    def driven(t, r, c):
        return dot(dv[t // 2, r, c, pl.ds(t % 2 * half, half)], wv[r, c, nstencil + nlinks])

    def nearby(total, r, c, near, shift):
        for k in range(nstencil):
            total = total + dot(near[r + shift + offs[0, k], c + 1 + offs[1, k]], wv[r, c, k])
        return total

    def distant(total, t, r, c):
        i = r * cols + c
        for l in range(nlinks):
            src = spot[level, ldev[g, l, 0, i] * LANES + lblk[g, l, 0, i]]
            total = total + dot(gaths[t][src], wv[r, c, nstencil + l])
        return total

    def renew(total, t, r, c):
        i = r * cols + c
        rate = leak[c, pl.ds(r, 1), :]
        old = owns[t][i].astype(jnp.float32)
        now = ((1.0 - rate) * old + rate * jnp.tanh(total)).astype(jnp.bfloat16)
        if t >= 2:
            xf[i, pl.ds((t - 2) * half, half)] = now
        else:
            owns[t + 2][i] = now

    def keep(i, total):
        acc[i] = total

    def gram_of(t, low, high):
        def one(i, carry):
            now = owns[t + 2][i] if t < 2 else xf[i, pl.ds(0, half)]
            r, c = i // cols, lax.rem(i, cols)
            gv[r, c] += lax.dot_general(now, now, (((0,), (0,)), ((), ())), preferred_element_type=jnp.float32)
            return carry

        lax.fori_loop(low, high, one, 0)

    loads, stores = [], []

    def finished(t, r):
        if t < 2:
            peer_copy(t + 2, r).start()
        if t == 3:
            stores.append(local(xf.at[pl.ds(r * cols, cols)], out.at[r], store_sem.at[1 + r]))

    for copy in firsts[0]:
        copy.wait()
    begin(0)
    for copy in firsts[1]:
        copy.wait()
    for r in range(rows):
        loads.append(local(w.at[r], wv.at[r], load_sem.at[4 + r]))
    loads.append(local(drive, dv, load_sem.at[4 + rows]))
    loads.append(local(gprev, gv, load_sem.at[5 + rows]))
    clear()
    follow(0)
    begin(1)
    for copy in loads:
        copy.wait()
    inner, outer = range(1, rows - 1), ((0, top, 1), (rows - 1, bot, 2 - rows))
    rims(0, rim_wait, False)
    fill_mid(0)
    for t in range(4):
        relay(t, 1)
        for r in inner:
            over(r, lambda c, i: keep(i, nearby(driven(t, r, c), r, c, mid, 0)))
        relay(t, 2)
        for r, _, _ in outer:
            over(r, lambda c, i: keep(i, driven(t, r, c)))
        if t in (1, 2):
            gram_of(t - 1, 0, cols)
            gram_of(t - 1, blocks - cols, blocks)
        settle(t)
        fill_rims(t)
        rims(t, lambda *at: rim_copy(*at).start(), True)
        for r in inner:
            over(r, lambda c, i: renew(distant(acc[i], t, r, c), t, r, c))
            finished(t, r)
        for r, _, _ in outer:
            over(r, lambda c, i: keep(i, distant(acc[i], t, r, c)))
        if t < 3:
            follow(t + 1)
        rims(t, rim_wait, True)
        fill_corners(t)
        for r, near, shift in outer:
            over(r, lambda c, i: renew(nearby(acc[i], r, c, near, shift), t, r, c))
            finished(t, r)
        if t < 3:
            rims(t + 1, rim_wait, False)
            fill_mid(t + 1)
        if t < 2:
            gram_of(t, cols, blocks - cols)
            for r in range(rows):
                peer_copy(t + 2, r).wait_recv()
            begin(t + 2)
        if t == 2:
            gram_of(t, 0, blocks)
        if t == 2:
            stores.append(local(gv, gout, store_sem.at[0]))
    for t in range(4):
        for link in (0, 1):
            for part_id in range(3):
                link_copy(t, link, part_id).wait_send()
                pass_copy(t, link, part_id).wait_send()
        rims(t, lambda *at: rim_copy(*at).wait_send(), False)
        rims(t, lambda *at: rim_copy(*at).wait_send(), True)
        if t >= 2:
            for r in range(rows):
                peer_copy(t, r).wait_send()
    for copy in stores:
        copy.wait()


def general(n_gy, state, weights, drive, leak, link_dev, link_blk, offsets, gram_prev):
    rows, cols, seq, units = state.shape
    blocks = rows * cols
    anywhere = pl.BlockSpec(memory_space=pl.ANY)
    scalars = pl.BlockSpec(memory_space=pltpu.SMEM)
    block = (seq // 2, units)
    return pl.pallas_call(
        functools.partial(reservoir, n_gy),
        out_shape=(
            jax.ShapeDtypeStruct(state.shape, state.dtype),
            jax.ShapeDtypeStruct(gram_prev.shape, gram_prev.dtype),
        ),
        in_specs=[
            anywhere, anywhere, anywhere, pl.BlockSpec(memory_space=pltpu.VMEM),
            scalars, scalars, scalars, anywhere,
        ],
        out_specs=(anywhere, anywhere),
        scratch_shapes=[
            *[pltpu.VMEM((8, blocks, *block), jnp.bfloat16)] * 4,
            *[pltpu.VMEM((rows + 2, cols + 2, *block), jnp.bfloat16)] * 4,
            pltpu.VMEM(weights.shape, weights.dtype),
            pltpu.VMEM(drive.shape, drive.dtype),
            pltpu.VMEM(gram_prev.shape, gram_prev.dtype),
            pltpu.VMEM((blocks, *block), jnp.float32),
            pltpu.VMEM((blocks, seq, units), jnp.bfloat16),
            pltpu.SemaphoreType.DMA((14,)),
            pltpu.SemaphoreType.DMA((8,)),
            pltpu.SemaphoreType.DMA((112,)),
            pltpu.SemaphoreType.DMA((4, 7, 4)),
            pltpu.SemaphoreType.DMA((4, 2, 6)),
            pltpu.SemaphoreType.DMA((4, 2, 6)),
        ],
        compiler_params=pltpu.CompilerParams(
            collective_id=0, has_side_effects=True, vmem_limit_bytes=62 * 1024 * 1024
        ),
    )(
        state, weights, drive, leak, link_dev, link_blk, offsets, gram_prev,
    )


def finish_gram(last, gram_part):
    rows = last.shape[0]
    state, gram_prev = last, gram_part
    anywhere = pl.BlockSpec(memory_space=pl.ANY)
    return pl.pallas_call(
        functools.partial(closing, last.shape[2] // 2),
        out_shape=(
            jax.ShapeDtypeStruct(state.shape, state.dtype),
            jax.ShapeDtypeStruct(gram_prev.shape, gram_prev.dtype),
        ),
        in_specs=[anywhere, anywhere],
        out_specs=(anywhere, anywhere),
        scratch_shapes=[
            pltpu.VMEM(state.shape, state.dtype),
            pltpu.VMEM(gram_prev.shape, gram_prev.dtype),
            *[pltpu.SemaphoreType.DMA((rows,))] * 4,
        ],
        compiler_params=pltpu.CompilerParams(vmem_limit_bytes=62 * 1024 * 1024),
    )(last, gram_part)


def listed(n_gy, level, peer, spot, pick, state, weights, drive, leak, link_dev, link_blk, offsets, gram_prev):
    rows, cols, seq, units = state.shape
    blocks = rows * cols
    anywhere = pl.BlockSpec(memory_space=pl.ANY)
    scalars = pl.BlockSpec(memory_space=pltpu.SMEM)
    slots, first = LEVELS[level]
    block = (seq // 2, units)
    held = lambda *n: pltpu.VMEM((*n, *block), jnp.bfloat16)
    copies = pltpu.SemaphoreType.DMA
    return pl.pallas_call(
        functools.partial(routed, n_gy, level),
        out_shape=(
            jax.ShapeDtypeStruct(state.shape, state.dtype),
            jax.ShapeDtypeStruct(gram_prev.shape, gram_prev.dtype),
        ),
        in_specs=[
            anywhere, anywhere, anywhere, anywhere, pl.BlockSpec(memory_space=pltpu.VMEM),
            scalars, scalars, scalars, scalars, scalars, anywhere,
        ],
        out_specs=(anywhere, anywhere),
        scratch_shapes=[
            *[held(2 * blocks)] * 4,
            *[held(2 * blocks + 4 * SLOTS)] * 4,
            *[held(AHEAD)] * 8,
            held(4, 2, first), held(4, 2, slots - first), held(4, 2, rows + 2), held(4, 2, 2),
            held(rows, cols + 2), held(3, cols + 2), held(3, cols + 2),
            pltpu.VMEM(weights.shape, weights.dtype),
            pltpu.VMEM(drive.shape, drive.dtype),
            pltpu.VMEM(gram_prev.shape, gram_prev.dtype),
            pltpu.VMEM((blocks, *block), jnp.float32),
            pltpu.VMEM((blocks, seq, units), jnp.bfloat16),
            copies((6 + rows,)), copies((1 + rows,)), copies((4, 3)),
            *[copies((4, 2, 3))] * 4,
            *[copies((2, rows))] * 2,
            *[copies((4, 2, rows + 2))] * 2,
        ],
        compiler_params=pltpu.CompilerParams(
            collective_id=2 + level, has_side_effects=True, vmem_limit_bytes=62 * 1024 * 1024
        ),
    )(
        state.reshape(blocks, seq, units), peer, weights, drive, leak, spot, pick,
        link_dev, link_blk, offsets, gram_prev,
    )


def fast_shards(n_gy, state, weights, drive, leak, link_dev, link_blk, offsets, gram_prev):
    rows, cols, seq, units = state.shape
    blocks = rows * cols
    anywhere = pl.BlockSpec(memory_space=pl.ANY)
    vector = pl.BlockSpec(memory_space=pltpu.VMEM)
    scalars = pl.BlockSpec(memory_space=pltpu.SMEM)
    ldev, lblk = link_dev.transpose(0, 3, 1, 2), link_blk.transpose(0, 3, 1, 2)
    table = lambda *n: jax.ShapeDtypeStruct((*n, 128), jnp.int32)
    spot, pick, verdict, peer = pl.pallas_call(
        functools.partial(agree, n_gy),
        out_shape=(
            table(8), table(len(LEVELS), 32), jax.ShapeDtypeStruct((1, 1), jnp.int32),
            jax.ShapeDtypeStruct((blocks, seq, units), state.dtype),
        ),
        in_specs=[scalars, scalars, anywhere],
        out_specs=(vector, vector, scalars, anywhere),
        scratch_shapes=[
            pltpu.VMEM((n_gy, 8, 128), jnp.int32),
            pltpu.SemaphoreType.DMA((n_gy,)),
            pltpu.SemaphoreType.DMA((n_gy,)),
        ],
        compiler_params=pltpu.CompilerParams(collective_id=1, has_side_effects=True),
    )(ldev, lblk, state.reshape(blocks, seq, units))
    operands = (state, weights, drive, leak.transpose(1, 0, 2), ldev, lblk, offsets.T, gram_prev)
    branches = [lambda: general(n_gy, *operands)]
    for level in range(len(LEVELS)):
        branches.append(functools.partial(listed, n_gy, level, peer, spot, pick, *operands))
    last, gram = lax.switch(verdict.reshape(()), branches)
    return finish_gram(last, gram)


def solution(mesh):
    part = shards
    if mesh.shape["gx"] == 8:
        part = functools.partial(fast_shards, mesh.shape["gy"])
    return jax.shard_map(
        part,
        mesh=mesh,
        in_specs=(
            P("gx", "gy", None, None),
            P("gx", "gy", None, None, None),
            P(None, "gx", "gy", None, None),
            P("gx", "gy", None),
            P(None, "gy", None, None),
            P(None, "gy", None, None),
            P(),
            P("gx", "gy", None, None),
        ),
        out_specs=(P("gx", "gy", None, None), P("gx", "gy", None, None)),
        check_vma=False,
    )
```
